128 devices in a mesh: ctx: 8 (over y_hi, x), exp: 16 (over y_lo, z, core).
Axes of the slice: x: 4, y: 4 (y_hi: 2, y_lo: 2; y = y_hi * 2 + y_lo), z: 4, core: 2. Of those that a mesh axis runs over, the one named last changes fastest.
Arguments:
- queries: bfloat16 [16, 1024, 2048], P('exp', 'ctx'), may hold values from -6 to 6
- key_rows: bfloat16 [16, 1024, 256], P('exp', 'ctx'), may hold values from -6 to 6
- value_matrix: bfloat16 [16, 1024, 256], P('exp', 'ctx'), may hold values from -4 to 4
- hidden: bfloat16 [16, 1024, 2880], P('exp', 'ctx'), may hold values from -30 to 30
- out_weight: bfloat16 [2048, 2880], P('ctx'), may hold values from -0.125 to 0.125
- norm_gain: float32 [2880], replicated, may hold values from 0.1 to 1.9
- block_order: int32 [16], replicated, may hold values from 0 to 15, each once
- expert_ids: int32 [16, 1024, 4], P('exp', 'ctx'), may hold values from 0 to 63, all different within a row; in each aligned block of 128 rows (0 to 127, 128 to 255, ..., all dimensions but the last counted through in order) at most 16 rows name the same one
- route_weights: float32 [16, 1024, 4], P('exp', 'ctx'), may hold values from 0.1 to 0.6
- gate_up_weight: bfloat16 [128, 2880, 1440], P(('ctx', 'exp')), may hold values from -0.109375 to 0.109375
- down_weight: bfloat16 [128, 720, 2880], P(('ctx', 'exp')), may hold values from -0.15625 to 0.15625
Outputs:
- layer_out: bfloat16 [16, 1024, 2880], P('exp', 'ctx')
The draws below stay inside these ranges and needn't reach their ends.
Inputs may be any that keep to these rules, and one draw needn't show every extreme that they name: `expert_ids`: the 128 rows of one device (aligned blocks of rows) name any one expert at most 16 times, a bound that some block reaches.
All inputs are finite; a program needn't handle non-finite values.
Results may differ from the reference program's by a relative error of at most 0.017.
Values may be sent and summed in bfloat16 or wider, within the bound.
A program may use at most 128 MiB of HBM per device.

```python
import math
import jax
import jax.numpy as jnp
import numpy as np
from jax import lax

D = 2880
QUERY_HEADS = 32
KEY_VALUE_HEADS = 4
HEAD_SIZE = 64
FF = 1440
TOPK = 4
BLK = 64
TOK_DEV = 128
SEQUENCE_LENGTH = 1024
FF_HALF = 720
EXPERTS = 64
CAP = 16
N_CTX = 8
N_EXP = 16


def drawn_fields(key):
    base = jax.random.fold_in(key, 11)
    key_layout_shape = (N_EXP, SEQUENCE_LENGTH, KEY_VALUE_HEADS, HEAD_SIZE)
    key_slice_field = jnp.clip(1.5 * jax.random.normal(jax.random.fold_in(base, 1), key_layout_shape, jnp.float32), -6.0, 6.0)
    query_slice_field = jnp.clip(1.5 * jax.random.normal(jax.random.fold_in(base, 2), (N_EXP, SEQUENCE_LENGTH, QUERY_HEADS * HEAD_SIZE), jnp.float32), -6.0, 6.0)
    return (query_slice_field, key_slice_field.reshape(N_EXP, SEQUENCE_LENGTH, KEY_VALUE_HEADS * HEAD_SIZE))


def draw_queries(key, part):
    return drawn_fields(key)[0].astype(jnp.bfloat16)


def draw_key_rows(key, part):
    return drawn_fields(key)[1].astype(jnp.bfloat16)


def draw_hidden(key, part):
    base = jax.random.fold_in(key, 23)
    shape = (N_EXP, SEQUENCE_LENGTH, D)
    field = jnp.clip(jax.random.normal(jax.random.fold_in(base, 1), shape, jnp.float32), -4.0, 4.0)
    row_scale = jnp.exp(jax.random.uniform(jax.random.fold_in(base, 3), (N_EXP, SEQUENCE_LENGTH, 1), jnp.float32, math.log(0.25), math.log(2.5)))
    col_scale = jnp.exp(jax.random.uniform(jax.random.fold_in(base, 4), (1, 1, D), jnp.float32, math.log(0.3), math.log(3.0)))
    return (field * row_scale * col_scale).astype(jnp.bfloat16)


def steps_of(own_key, extent, split, least, top_value):
    def one(axis_at, blocks):
        draws = jax.random.uniform(jax.random.fold_in(jax.random.fold_in(own_key, 6), axis_at), (blocks,), jnp.float32, least / len(split), top_value / len(split))
        return jnp.repeat(jnp.exp(draws), extent[axis_at] // blocks).reshape((-1,) + (1,) * (len(extent) - axis_at - 1))

    factor_of = one(*split[0])
    for cut in split[1:]:
        factor_of = factor_of * one(*cut)
    return factor_of


def routed_block(own_key, own, number, rows, number_of, top, reach, skew):
    ranking = jax.random.permutation(own_key, number_of)
    crowded, ordinary = load_shares(number_of, rows * top, reach, skew, True), load_shares(number_of, rows * top, reach, skew, False)
    places = jnp.arange(number_of)

    def named(tallies, turn):
        used = int((tallies > 0).sum())
        fixed = max(1, used // 4)
        passed = fixed + (places - fixed + turn * (used - fixed)) % max(1, number_of - fixed)
        return jnp.zeros((number_of,), jnp.int32).at[ranking[jnp.where(places < fixed, places, passed)]].set(jnp.asarray(tallies, jnp.int32))

    tallies = jnp.where(number % 4 == 0, named(crowded, number // 4), named(ordinary, number - number // 4 - 1))
    mixed = jax.random.permutation(jax.random.fold_in(own, 3), number_of)
    donor, sink = mixed[0:number_of // 2 * 2:2], mixed[1:number_of // 2 * 2:2]
    slack = jnp.minimum(tallies[donor] - 1, reach - tallies[sink]) // 2
    slack = jnp.where((donor == ranking[0]) | (sink == ranking[0]) | (tallies[sink] == 0), 0, jnp.maximum(slack, 0))
    passed = jax.random.randint(jax.random.fold_in(own, 4), (number_of // 2,), 0, 1 << 20) % (slack + 1)
    tallies = tallies.at[donor].add(-passed).at[sink].add(passed)
    members = jnp.searchsorted(jnp.cumsum(tallies), jnp.arange(rows * top), side="right").astype(jnp.int32)
    listing = members.reshape(top, rows).T
    listing = listing[jax.random.permutation(jax.random.fold_in(own, 1), rows)]
    turn = jax.random.randint(jax.random.fold_in(own, 2), (rows, 1), 0, top)
    return jnp.take_along_axis(listing, (jnp.arange(top)[None, :] + turn) % top, axis=1)


def load_shares(amount, total, most, slope, full):
    portions = [(1 << 20) // math.isqrt(rank ** slope) + 1 for rank in range(1, amount + 1)]
    largest = most if full else min(most, max(-(-total // amount), total * portions[0] // sum(portions)))
    least = 1 if total - largest >= amount - 1 else 0
    counts, rest = [largest] + [least] * (amount - 1), total - largest - least * (amount - 1)
    while rest > 0:
        candidates = [i for i in range(1, amount) if counts[i] < largest] or [i for i in range(1, amount) if counts[i] < most]
        mass, remaining = sum([portions[i] for i in candidates]), rest
        for i in candidates:
            addition = min(most - counts[i], max(1, remaining * portions[i] // mass), rest)
            counts[i] = counts[i] + addition
            rest = rest - addition
    return np.array(counts)


def bell_draw(rng, dims, width, reach, pieces=(), held_as=jnp.bfloat16):
    entries = jax.random.normal(rng, dims, jnp.float32) * width
    if len(pieces) > 0:
        entries = steps_of(rng, dims, pieces, -0.22, 0.18) * entries
    return jnp.clip(entries, min=-reach, max=reach).astype(held_as)


def setup_inputs(seed: int = 0) -> dict:
    splits = jax.random.split(jax.random.key(seed), 12)
    queries = draw_queries(jax.random.fold_in(splits[11], 71), 0)
    key_rows = draw_key_rows(jax.random.fold_in(splits[11], 71), 0)
    value_matrix = bell_draw(splits[2], (N_EXP, SEQUENCE_LENGTH, KEY_VALUE_HEADS * HEAD_SIZE), 1.0, 4.0, ((0, 16), (1, 8)))
    hidden = draw_hidden(jax.random.fold_in(splits[11], 71), 0)
    out_weight = bell_draw(splits[4], (QUERY_HEADS * HEAD_SIZE, D), (QUERY_HEADS * HEAD_SIZE) ** -0.5, 0.125, ((0, 8),))
    norm_gain = jnp.clip(1.0 + 0.18 * jax.random.normal(splits[5], (D,), jnp.float32), 0.1, 1.9)
    block_order = jax.random.permutation(splits[6], 2 * N_CTX).astype(jnp.int32)
    expert_ids_keys = jax.random.split(jax.random.fold_in(splits[7], 1), N_EXP * SEQUENCE_LENGTH // TOK_DEV)
    expert_ids_turns = jax.random.permutation(jax.random.fold_in(splits[7], 3), N_EXP * SEQUENCE_LENGTH // TOK_DEV)
    expert_ids = jax.vmap(lambda own, number: routed_block(jax.random.fold_in(splits[7], 2), own, number, TOK_DEV, EXPERTS, TOPK, CAP, 2))(expert_ids_keys, expert_ids_turns).reshape((N_EXP, SEQUENCE_LENGTH, TOPK))
    route_weights = jnp.clip(0.1 + 0.5 * jax.random.uniform(splits[8], (N_EXP, SEQUENCE_LENGTH, TOPK), jnp.float32) ** steps_of(splits[8], (N_EXP, SEQUENCE_LENGTH, TOPK), ((0, 16), (1, 8)), -0.2, 0.2), 0.1, 0.6)
    gate_up_weight = bell_draw(splits[9], (2 * EXPERTS, D, 2 * FF_HALF), D ** -0.5, 0.109375, ((0, 128),))
    down_weight = bell_draw(splits[10], (2 * EXPERTS, FF_HALF, D), FF ** -0.5, 0.15625, ((0, 128),))
    return dict(queries=queries, key_rows=key_rows, value_matrix=value_matrix, hidden=hidden, out_weight=out_weight, norm_gain=norm_gain, block_order=block_order, expert_ids=expert_ids, route_weights=route_weights, gate_up_weight=gate_up_weight, down_weight=down_weight)


negative_large = -1e+30

def positions_of(block_order):
    row_index = jnp.arange(SEQUENCE_LENGTH, dtype=jnp.int32)
    return block_order[row_index // BLK] * BLK + row_index % BLK

def attend_sequence(query_sequence, key_sequence, value_sequence, positions):
    query_group_size = QUERY_HEADS // KEY_VALUE_HEADS
    query_head_rows = query_sequence.astype(jnp.float32).reshape(SEQUENCE_LENGTH, KEY_VALUE_HEADS, query_group_size, HEAD_SIZE)
    key_head_rows = key_sequence.astype(jnp.float32).reshape(SEQUENCE_LENGTH, KEY_VALUE_HEADS, HEAD_SIZE)
    value_head_rows = value_sequence.astype(jnp.float32).reshape(SEQUENCE_LENGTH, KEY_VALUE_HEADS, HEAD_SIZE)
    scores = jnp.einsum('qhgd,khd->hgqk', query_head_rows, key_head_rows) * HEAD_SIZE ** (-0.5)
    visible = positions[None, :] <= positions[:, None]
    masked = jnp.where(visible, scores, negative_large)
    row_maximum = lax.optimization_barrier(jnp.max(masked, axis=-1, keepdims=True))
    kept_probs = jnp.where(visible, jnp.exp(masked - row_maximum), 0.0)
    row_total = lax.optimization_barrier(jnp.sum(kept_probs, axis=-1))
    probs_low = kept_probs.astype(jnp.bfloat16)
    weighted_sum = jnp.einsum('hgqk,khd->qhgd', probs_low.astype(jnp.float32), value_head_rows)
    attended = weighted_sum / jnp.transpose(row_total, (2, 0, 1))[..., None]
    return attended.reshape(SEQUENCE_LENGTH, QUERY_HEADS * HEAD_SIZE).astype(jnp.bfloat16)

def expert_half(routed, gate_up, down_part):
    gate_up_out = jnp.dot(routed, gate_up, preferred_element_type=jnp.float32)
    gate_part = gate_up_out[:, :FF_HALF]
    up_part = gate_up_out[:, FF_HALF:]
    activated = (gate_part * jax.nn.sigmoid(1.702 * gate_part) * (up_part + 1.0)).astype(jnp.bfloat16)
    return jnp.dot(activated, down_part, preferred_element_type=jnp.float32).astype(jnp.bfloat16)

def reference(queries, key_rows, value_matrix, hidden, out_weight, norm_gain, block_order, expert_ids, route_weights, gate_up_weight, down_weight):
    positions = positions_of(block_order)
    attended = lax.map(lambda triple: attend_sequence(triple[0], triple[1], triple[2], positions), (queries, key_rows, value_matrix))
    projected = jnp.dot(attended.reshape(-1, QUERY_HEADS * HEAD_SIZE), out_weight, preferred_element_type=jnp.float32)
    residual = (hidden.reshape(-1, D).astype(jnp.float32) + projected).astype(jnp.bfloat16)
    res_float = residual.astype(jnp.float32)
    moe_in = (res_float * lax.rsqrt(lax.optimization_barrier(jnp.mean(res_float * res_float, axis=-1, keepdims=True)) + 1e-05) * norm_gain).astype(jnp.bfloat16)
    flat_ids = expert_ids.reshape(-1)
    flat_weights = route_weights.reshape(-1)
    limit = N_EXP * N_CTX * CAP

    def one_expert(moe_total, expert):
        matches = flat_ids == expert
        picked = jnp.nonzero(matches, size=limit, fill_value=0)[0].astype(jnp.int32)
        is_valid = jnp.arange(limit, dtype=jnp.int32) < jnp.sum(matches.astype(jnp.int32))
        tokens = picked // TOPK
        weights_now = jnp.where(is_valid, flat_weights[picked], 0.0)
        routed = moe_in[tokens]
        first_half = expert_half(routed, gate_up_weight[2 * expert], down_weight[2 * expert]).astype(jnp.float32)
        second_half = expert_half(routed, gate_up_weight[2 * expert + 1], down_weight[2 * expert + 1]).astype(jnp.float32)
        combined = (first_half + second_half).astype(jnp.bfloat16).astype(jnp.float32)
        return (moe_total.at[tokens].add(weights_now[:, None] * combined), None)
    moe_total, _ = lax.scan(one_expert, jnp.zeros((N_EXP * SEQUENCE_LENGTH, D), jnp.float32), jnp.arange(EXPERTS, dtype=jnp.int32))
    return (res_float + moe_total).astype(jnp.bfloat16).reshape(N_EXP, SEQUENCE_LENGTH, D)
```

```python
import jax
import jax.numpy as jnp
from jax import lax
from jax.sharding import Mesh, PartitionSpec as P

D = 2880
QUERY_HEADS = 32
KEY_VALUE_HEADS = 4
HEAD_SIZE = 64
TOPK = 4
EXPERTS = 64
CAP = 16

CTX = ("y_hi", "x")
EXP = ("y_lo", "z", "core")
CHIPS = ("y_hi", "x", "y_lo", "z")

negative_large = -1e30


def attention(queries, key_rows, value_matrix, block_order):
    token_count = queries.shape[1]
    block_len = token_count // 2
    group = QUERY_HEADS // KEY_VALUE_HEADS
    slot_ids = jnp.arange(16, dtype=jnp.int32)

    def locate(row_index):
        table = (row_index // block_len)[:, None] == slot_ids[None, :]
        return (
            jnp.sum(jnp.where(table, block_order[None, :], 0), axis=1) * block_len
            + row_index % block_len
        )

    query_pos = locate(
        lax.axis_index(CTX) * token_count + jnp.arange(token_count, dtype=jnp.int32)
    )
    query_head_rows = queries[0].reshape(token_count, KEY_VALUE_HEADS, group, HEAD_SIZE)
    both = lax.all_gather(
        jnp.concatenate([key_rows[0], value_matrix[0]], axis=1), CTX, axis=0, tiled=True
    )
    section_length = both.shape[0]
    key_pos = locate(jnp.arange(section_length, dtype=jnp.int32))
    kv = both.reshape(section_length, 2, KEY_VALUE_HEADS, HEAD_SIZE)
    key_head_rows, value_head_rows = kv[:, 0], kv[:, 1]
    scores = jnp.einsum(
        "qhgd,khd->hgqk", query_head_rows, key_head_rows, preferred_element_type=jnp.float32
    ) * HEAD_SIZE ** (-0.5)
    visible = key_pos[None, :] <= query_pos[:, None]
    masked = jnp.where(visible, scores, negative_large)
    new_max = jnp.max(masked, axis=-1)
    kept_probs = jnp.where(visible, jnp.exp(masked - new_max[..., None]), 0.0)
    row_total = jnp.sum(kept_probs, axis=-1)
    added = jnp.einsum(
        "hgqk,khd->qhgd",
        kept_probs.astype(jnp.bfloat16),
        value_head_rows,
        preferred_element_type=jnp.float32,
    )
    return (
        (added / jnp.transpose(row_total, (2, 0, 1))[..., None])
        .astype(jnp.bfloat16)
        .reshape(token_count, QUERY_HEADS * HEAD_SIZE)
    )


def local(
    queries,
    key_rows,
    value_matrix,
    hidden,
    out_weight,
    norm_gain,
    block_order,
    expert_ids,
    route_weights,
    gate_up_weight,
    down_weight,
):
    swap = [(0, 1), (1, 0)]
    gate_up_own, down_own = gate_up_weight[0], down_weight[0]
    gate_up_oth = lax.ppermute(gate_up_own, "core", swap)
    down_oth = lax.ppermute(down_own, "core", swap)

    attended = attention(queries, key_rows, value_matrix, block_order)
    projected = jnp.dot(
        attended,
        lax.all_gather(out_weight, CTX, axis=0, tiled=True),
        preferred_element_type=jnp.float32,
    )
    residual = (hidden[0].astype(jnp.float32) + projected).astype(jnp.bfloat16)
    res_float = residual.astype(jnp.float32)
    moe_in = (
        res_float
        * lax.rsqrt(jnp.mean(res_float * res_float, axis=-1, keepdims=True) + 1e-05)
        * norm_gain
    ).astype(jnp.bfloat16)

    ids, weights = expert_ids[0], route_weights[0]
    token_count = ids.shape[0]
    named = ids[:, :, None] == jnp.arange(EXPERTS, dtype=jnp.int32)
    member = jnp.any(named, axis=1)
    weight_of = jnp.sum(jnp.where(named, weights[:, :, None], 0.0), axis=1)
    tok = jnp.arange(token_count, dtype=jnp.int32)
    before = (tok[None, :] < tok[:, None]).astype(jnp.bfloat16)
    slot = jnp.dot(
        before, member.astype(jnp.bfloat16), preferred_element_type=jnp.float32
    ).astype(jnp.int32)
    place = (
        member.T[:, None, :]
        & (slot.T[:, None, :] == jnp.arange(CAP, dtype=jnp.int32)[None, :, None])
    ).reshape(EXPERTS * CAP, token_count)
    picked = place.astype(jnp.bfloat16)
    spread = jnp.where(
        place, jnp.broadcast_to(weight_of.T[:, None, :], (EXPERTS, CAP, token_count)).reshape(EXPERTS * CAP, token_count), 0.0
    )
    high = spread.astype(jnp.bfloat16)
    low = (spread - high.astype(jnp.float32)).astype(jnp.bfloat16)

    outgoing = jnp.dot(picked, moe_in, preferred_element_type=jnp.float32).astype(jnp.bfloat16)
    rows = lax.all_to_all(
        outgoing.reshape(EXPERTS, CAP, D), CHIPS, split_axis=0, concat_axis=0, tiled=True
    ).reshape(EXPERTS * CAP, D)

    def half(gate_up, down):
        gate_up_out = jnp.dot(rows, gate_up, preferred_element_type=jnp.float32)
        n = gate_up.shape[1] // 2
        gate, up = gate_up_out[:, :n], gate_up_out[:, n:]
        act = (gate * jax.nn.sigmoid(1.702 * gate) * (up + 1.0)).astype(jnp.bfloat16)
        return jnp.dot(act, down, preferred_element_type=jnp.float32)

    result = (half(gate_up_own, down_own) + half(gate_up_oth, down_oth)).astype(jnp.bfloat16)
    returned = lax.all_to_all(
        result.reshape(EXPERTS, CAP, D), CHIPS, split_axis=0, concat_axis=0, tiled=True
    ).reshape(EXPERTS * CAP, D)
    mixed = jnp.einsum("st,sd->td", high, returned, preferred_element_type=jnp.float32) + jnp.einsum(
        "st,sd->td", low, returned, preferred_element_type=jnp.float32
    )
    return (res_float + mixed).astype(jnp.bfloat16)[None]


def solution(mesh):
    fine = Mesh(mesh.devices.reshape(2, 4, 2, 4, 2), ("y_hi", "x", "y_lo", "z", "core"))
    rows = P(EXP, CTX, None)
    halves = P(CTX + EXP, None, None)
    return jax.shard_map(
        local,
        mesh=fine,
        in_specs=(
            rows, rows, rows, rows, P(CTX, None), P(), P(), rows, rows, halves, halves,
        ),
        out_specs=rows,
        check_vma=False,
    )
```

```python
import functools
import jax
import jax.numpy as jnp
from jax import lax
from jax.experimental import pallas as pl
from jax.experimental.pallas import tpu as pltpu
from jax.sharding import Mesh, PartitionSpec as P

D = 2880
HALF_D = D // 2
HEAD = 64
TOK = 128
QUARTER = 224
REST = HALF_D - 4 * QUARTER
AXES = ("y_hi", "x", "y_lo", "z", "core")
MESH = pl.DeviceIdType.MESH


def here():
    return {a: lax.axis_index(a) for a in AXES}


def moved(me, axis, by):
    to = dict(me)
    if axis == "y":
        y = (me["y_hi"] * 2 + me["y_lo"] + by) % 4
        to["y_hi"], to["y_lo"] = y // 2, y % 2
    else:
        to[axis] = (me[axis] + by) % 4
    return to


class Copies:
    def __init__(self, send, recv):
        self.send, self.recv, self.made = send, recv, []

    def go(self, src, dst, to):
        i = len(self.made)
        c = pltpu.make_async_remote_copy(
            src_ref=src, dst_ref=dst, send_sem=self.send.at[i], recv_sem=self.recv.at[i],
            device_id=to, device_id_type=MESH,
        )
        c.start()
        self.made.append(c)
        return c

    def drain(self):
        for c in self.made:
            c.wait_send()


def greet(peers):
    barrier = pltpu.get_barrier_semaphore()
    for peer in peers:
        pl.semaphore_signal(barrier, inc=1, device_id=peer, device_id_type=MESH)
    pl.semaphore_wait(barrier, len(peers))


FRONT_COPIES = 80


def front_kernel(
    order, q, k, v, hid, gain, ow, gu, dn,
    residual, moe_in, gu_oth, dn_oth,
    kv, w, att, acc, got, send, recv, local_sem,
):
    me = here()
    cp = Copies(send, recv)
    core = me["core"]
    other = dict(me, core=1 - core)
    kv_mate = dict(me, y_hi=1 - me["y_hi"])
    w_mate = dict(me, y_hi=1 - me["y_hi"], y_lo=1 - me["y_lo"])
    xp, xm = moved(me, "x", 1), moved(me, "x", 3)
    zp, zm = moved(me, "z", 1), moved(me, "z", 3)
    z = me["z"]
    base = pl.multiple_of(core * HALF_D, 16)
    greet([other, kv_mate, w_mate, xp, xm, zp, zm])

    def quarter(t, part=None):
        start = REST + QUARTER * ((z + t) % 4)
        size = QUARTER
        if part is not None:
            size = QUARTER // 2
            start = start + part * size
        return pl.ds(pl.multiple_of(start, 16), size)

    own_q = ow.at[pl.ds(pl.multiple_of(base + REST + QUARTER * z, 16), QUARTER)]
    own_r = ow.at[pl.ds(base, REST)]
    rest = pl.ds(0, REST)
    rest_parts = (pl.ds(0, REST // 2), pl.ds(REST // 2, REST // 2))

    own_w = pltpu.make_async_copy(ow.at[pl.ds(base, HALF_D)], w.at[0], local_sem.at[0])
    own_w.start()
    kv[0, :, pl.ds(0, 256)] = k[...]
    kv[0, :, pl.ds(256, 256)] = v[...]

    yq = cp.go(own_q, w.at[4, quarter(0)], w_mate)
    xq = {0: (cp.go(own_q, w.at[3, quarter(0)], xp), cp.go(own_q, w.at[1, quarter(0)], xm))}
    ky = cp.go(kv.at[0], kv.at[4], kv_mate)
    kx = {0: (cp.go(kv.at[0], kv.at[3], xp), cp.go(kv.at[0], kv.at[1], xm))}
    yr = cp.go(own_r, w.at[4, rest], w_mate)
    xr = {0: (cp.go(own_r, w.at[3, rest], xp), cp.go(own_r, w.at[1, rest], xm))}
    swaps = [cp.go(gu, gu_oth, other), cp.go(dn, dn_oth, other)]
    zq, zq2 = {}, {}

    def z_first(slot):
        rows = quarter(0)
        zq[slot] = (
            cp.go(w.at[slot, rows], w.at[slot, rows], zp),
            cp.go(w.at[slot, rows], w.at[slot, rows], zm),
        )

    def z_second(slot):
        zq[slot][0].wait_recv()
        a = w.at[slot, quarter(3, 0)]
        zq[slot][1].wait_recv()
        b = w.at[slot, quarter(1, 1)]
        zq2[slot] = (cp.go(a, a, zp), cp.go(b, b, zm))

    def x_second(buf, d, firsts, parts):
        for c in firsts:
            c.wait_recv()
        return (
            cp.go(buf.at[4 * d + 3, parts[0]], buf.at[4 * d + 2, parts[0]], xp),
            cp.go(buf.at[4 * d + 1, parts[1]], buf.at[4 * d + 2, parts[1]], xm),
        )

    kv_parts = (pl.ds(0, 64), pl.ds(64, 64))
    q_parts = (quarter(0, 0), quarter(0, 1))
    yq.wait_recv()
    xq[1] = (
        cp.go(w.at[4, quarter(0)], w.at[7, quarter(0)], xp),
        cp.go(w.at[4, quarter(0)], w.at[5, quarter(0)], xm),
    )
    z_first(4)
    x2q = {0: x_second(w, 0, xq[0], q_parts)}
    z_first(3)
    z_first(1)
    ky.wait_recv()
    kx[1] = (cp.go(kv.at[4], kv.at[7], xp), cp.go(kv.at[4], kv.at[5], xm))
    kx2 = {0: x_second(kv, 0, kx[0], kv_parts)}
    x2q[1] = x_second(w, 1, xq[1], q_parts)
    z_first(7)
    z_first(5)
    kx2[1] = x_second(kv, 1, kx[1], kv_parts)
    for c in x2q[0]:
        c.wait_recv()
    z_first(2)
    for c in x2q[1]:
        c.wait_recv()
    z_first(6)
    z_second(4)
    yr.wait_recv()
    xr[1] = (cp.go(w.at[4, rest], w.at[7, rest], xp), cp.go(w.at[4, rest], w.at[5, rest], xm))
    for d in (0, 1):
        for c in kx2[d]:
            c.wait_recv()

    ctx = me["y_hi"] * 4 + me["x"]
    col = lax.broadcasted_iota(jnp.int32, (1, 1024), 1)
    key_pos = col % 64
    for slot in range(8):
        block = ((me["y_hi"] + slot // 4) % 2) * 4 + (me["x"] + slot % 4) % 4
        for h in (0, 1):
            key_pos = key_pos + jnp.where(
                col // 64 == 2 * slot + h, order[2 * block + h] * 64, 0
            )
    row = lax.broadcasted_iota(jnp.int32, (256, 1), 0) % TOK
    query_pos = row % 64 + jnp.where(row < 64, order[2 * ctx] * 64, order[2 * ctx + 1] * 64)
    bias = jnp.where(key_pos <= query_pos, 0.0, -1e30)

    def group(g):
        keys = kv[:, :, 64 * g : 64 * g + 64].reshape(1024, HEAD)
        values = kv[:, :, 256 + 64 * g : 256 + 64 * g + 64].reshape(1024, HEAD)

        def pair(i, _):
            lanes = pl.ds(pl.multiple_of((4 * g + i) * 128, 128), 128)
            two = q[:, lanes] * jnp.bfloat16(0.125)
            two = jnp.concatenate([two[:, :HEAD], two[:, HEAD:]], axis=0)
            s = lax.dot_general(
                two, keys, (((1,), (1,)), ((), ())), preferred_element_type=jnp.float32
            ) + bias
            p = jnp.exp(s - jnp.max(s, axis=1, keepdims=True))
            total = jnp.sum(p, axis=1, keepdims=True)
            o = jnp.dot(p.astype(jnp.bfloat16), values, preferred_element_type=jnp.float32)
            o = (o / total).astype(jnp.bfloat16)
            att[0, :, lanes] = jnp.concatenate([o[:TOK], o[TOK:]], axis=1)
            return 0

        lax.fori_loop(0, 4, pair, 0)

    group(0)
    z_second(3)
    z_second(1)
    x2r = {0: x_second(w, 0, xr[0], rest_parts)}
    group(1)
    z_second(7)
    z_second(5)
    group(2)
    x2r[1] = x_second(w, 1, xr[1], rest_parts)
    z_second(2)
    z_second(6)
    group(3)
    att_out = cp.go(att.at[0], att.at[1], other)
    own_w.wait()
    att_out.wait_recv()

    def project(slot, first=False):
        block = ((me["y_hi"] + slot // 4) % 2) * 4 + (me["x"] + slot % 4) % 4
        lanes = pl.ds(pl.multiple_of(block * 256, 256), 256)
        both = att[:, :, lanes].reshape(2 * TOK, 256)
        part = lax.dot_general(
            both, w[slot], (((1,), (1,)), ((), ())), preferred_element_type=jnp.float32
        ).reshape(2, TOK, HALF_D)
        acc[...] = part if first else acc[...] + part

    project(0, True)
    for slot in (4, 3, 1, 7, 5, 2, 6):
        d, s = slot // 4, slot % 4
        if slot == 4:
            pass
        elif s == 2:
            for c in x2r[d]:
                c.wait_recv()
        for c in zq2[slot]:
            c.wait_recv()
        project(slot)
    back = cp.go(acc.at[1], got, other)
    hidden = hid[...].astype(jnp.float32)
    back.wait_recv()
    mine, theirs = acc[0], got[...]
    left = jnp.where(core == 0, mine, theirs)
    right = jnp.where(core == 0, theirs, mine)
    res = (hidden + jnp.concatenate([left, right], axis=1)).astype(jnp.bfloat16)
    residual[...] = res
    res = res.astype(jnp.float32)
    scale = lax.rsqrt(jnp.mean(res * res, axis=1, keepdims=True) + 1e-05)
    moe_in[...] = (res * scale * gain[...]).astype(jnp.bfloat16)
    for c in swaps:
        c.wait_recv()
    cp.drain()


def front(q, k, v, hidden, gain, ow_t, order, gu_t, dn):
    vmem, anyspace = pl.BlockSpec(memory_space=pltpu.VMEM), pl.BlockSpec(memory_space=pl.ANY)
    bf = jnp.bfloat16
    return pl.pallas_call(
        front_kernel,
        out_shape=(
            jax.ShapeDtypeStruct((TOK, D), bf), jax.ShapeDtypeStruct((TOK, D), bf),
            jax.ShapeDtypeStruct(gu_t.shape, bf), jax.ShapeDtypeStruct(dn.shape, bf),
        ),
        in_specs=[pl.BlockSpec(memory_space=pltpu.SMEM), vmem, vmem, vmem, vmem, vmem, anyspace, anyspace, anyspace],
        out_specs=(vmem, vmem, anyspace, anyspace),
        scratch_shapes=[
            pltpu.VMEM((8, TOK, 512), bf),
            pltpu.VMEM((8, HALF_D, 256), bf),
            pltpu.VMEM((2, TOK, 2048), bf),
            pltpu.VMEM((2, TOK, HALF_D), jnp.float32),
            pltpu.VMEM((TOK, HALF_D), jnp.float32),
            pltpu.SemaphoreType.DMA((FRONT_COPIES,)),
            pltpu.SemaphoreType.DMA((FRONT_COPIES,)),
            pltpu.SemaphoreType.DMA((1,)),
        ],
        compiler_params=pltpu.CompilerParams(
            collective_id=0, has_side_effects=True, vmem_limit_bytes=48 * 2**20
        ),
    )(order, q, k, v, hidden, gain, ow_t, gu_t, dn)


TOPK = 4
EXPERTS = 64
CAP = 16

CTX = ("y_hi", "x")
EXP = ("y_lo", "z", "core")
CHIPS = ("y_hi", "x", "y_lo", "z")


def local(
    queries,
    key_rows,
    value_matrix,
    hidden,
    out_weight,
    norm_gain,
    block_order,
    expert_ids,
    route_weights,
    gate_up_weight,
    down_weight,
):
    gate_up_own, down_own = gate_up_weight[0].T, down_weight[0]
    residual, moe_in, gate_up_oth, down_oth = front(
        queries[0], key_rows[0], value_matrix[0], hidden[0], norm_gain[None], out_weight.T,
        block_order, gate_up_own, down_own,
    )
    gate_up_own, gate_up_oth = gate_up_own.T, gate_up_oth.T
    res_float = residual.astype(jnp.float32)

    ids, weights = expert_ids[0], route_weights[0]
    token_count = ids.shape[0]
    named = ids[:, :, None] == jnp.arange(EXPERTS, dtype=jnp.int32)
    member = jnp.any(named, axis=1)
    weight_of = jnp.sum(jnp.where(named, weights[:, :, None], 0.0), axis=1)
    tok = jnp.arange(token_count, dtype=jnp.int32)
    before = (tok[None, :] < tok[:, None]).astype(jnp.bfloat16)
    slot = jnp.dot(
        before, member.astype(jnp.bfloat16), preferred_element_type=jnp.float32
    ).astype(jnp.int32)
    place = (
        member.T[:, None, :]
        & (slot.T[:, None, :] == jnp.arange(CAP, dtype=jnp.int32)[None, :, None])
    ).reshape(EXPERTS * CAP, token_count)
    picked = place.astype(jnp.bfloat16)
    spread = jnp.where(
        place, jnp.broadcast_to(weight_of.T[:, None, :], (EXPERTS, CAP, token_count)).reshape(EXPERTS * CAP, token_count), 0.0
    )
    high = spread.astype(jnp.bfloat16)
    low = (spread - high.astype(jnp.float32)).astype(jnp.bfloat16)

    outgoing = jnp.dot(picked, moe_in, preferred_element_type=jnp.float32).astype(jnp.bfloat16)
    rows = lax.all_to_all(
        outgoing.reshape(EXPERTS, CAP, D), CHIPS, split_axis=0, concat_axis=0, tiled=True
    ).reshape(EXPERTS * CAP, D)

    def half(gate_up, down):
        gate_up_out = jnp.dot(rows, gate_up, preferred_element_type=jnp.float32)
        n = gate_up.shape[1] // 2
        gate, up = gate_up_out[:, :n], gate_up_out[:, n:]
        act = (gate * jax.nn.sigmoid(1.702 * gate) * (up + 1.0)).astype(jnp.bfloat16)
        return jnp.dot(act, down, preferred_element_type=jnp.float32)

    result = (half(gate_up_own, down_own) + half(gate_up_oth, down_oth)).astype(jnp.bfloat16)
    returned = lax.all_to_all(
        result.reshape(EXPERTS, CAP, D), CHIPS, split_axis=0, concat_axis=0, tiled=True
    ).reshape(EXPERTS * CAP, D)
    mixed = jnp.einsum("st,sd->td", high, returned, preferred_element_type=jnp.float32) + jnp.einsum(
        "st,sd->td", low, returned, preferred_element_type=jnp.float32
    )
    return (res_float + mixed).astype(jnp.bfloat16)[None]


def solution(mesh):
    fine = Mesh(mesh.devices.reshape(2, 4, 2, 4, 2), ("y_hi", "x", "y_lo", "z", "core"))
    rows = P(EXP, CTX, None)
    halves = P(CTX + EXP, None, None)
    return jax.shard_map(
        local,
        mesh=fine,
        in_specs=(
            rows, rows, rows, rows, P(CTX, None), P(), P(), rows, rows, halves, halves,
        ),
        out_specs=rows,
        check_vma=False,
    )
```

```python
import functools
import jax
import jax.numpy as jnp
from jax import lax
from jax.experimental import pallas as pl
from jax.experimental.pallas import tpu as pltpu
from jax.sharding import Mesh, PartitionSpec as P

D = 2880
HALF_D = D // 2
HEAD = 64
TOK = 128
QUARTER = 224
REST = HALF_D - 4 * QUARTER
AXES = ("y_hi", "x", "y_lo", "z", "core")
MESH = pl.DeviceIdType.MESH
CTX = ("y_hi", "x")
EXP = ("y_lo", "z", "core")


def here():
    return {a: lax.axis_index(a) for a in AXES}


def moved(me, axis, by):
    to = dict(me)
    if axis == "y":
        y = (me["y_hi"] * 2 + me["y_lo"] + by) % 4
        to["y_hi"], to["y_lo"] = y // 2, y % 2
    else:
        to[axis] = (me[axis] + by) % 4
    return to


class Copies:
    def __init__(self, send, recv):
        self.send, self.recv, self.made = send, recv, []

    def go(self, src, dst, to):
        i = len(self.made)
        c = pltpu.make_async_remote_copy(
            src_ref=src, dst_ref=dst, send_sem=self.send.at[i], recv_sem=self.recv.at[i],
            device_id=to, device_id_type=MESH,
        )
        c.start()
        self.made.append(c)
        return c

    def drain(self):
        for c in self.made:
            c.wait_send()


def greet(peers):
    barrier = pltpu.get_barrier_semaphore()
    for peer in peers:
        pl.semaphore_signal(barrier, inc=1, device_id=peer, device_id_type=MESH)
    pl.semaphore_wait(barrier, len(peers))


FRONT_COPIES = 80


def front_kernel(
    order, q, k, v, hid, gain, ow, gu, dn,
    residual, moe_in, gu_oth, dn_oth,
    kv, w, att, acc, got, send, recv, local_sem,
):
    me = here()
    cp = Copies(send, recv)
    core = me["core"]
    other = dict(me, core=1 - core)
    kv_mate = dict(me, y_hi=1 - me["y_hi"])
    w_mate = dict(me, y_hi=1 - me["y_hi"], y_lo=1 - me["y_lo"])
    xp, xm = moved(me, "x", 1), moved(me, "x", 3)
    zp, zm = moved(me, "z", 1), moved(me, "z", 3)
    z = me["z"]
    base = pl.multiple_of(core * HALF_D, 16)
    greet([other, kv_mate, w_mate, xp, xm, zp, zm])

    def quarter(t, part=None):
        start = REST + QUARTER * ((z + t) % 4)
        size = QUARTER
        if part is not None:
            size = QUARTER // 2
            start = start + part * size
        return pl.ds(pl.multiple_of(start, 16), size)

    own_q = ow.at[pl.ds(pl.multiple_of(base + REST + QUARTER * z, 16), QUARTER)]
    own_r = ow.at[pl.ds(base, REST)]
    rest = pl.ds(0, REST)
    rest_parts = (pl.ds(0, REST // 2), pl.ds(REST // 2, REST // 2))

    own_w = pltpu.make_async_copy(ow.at[pl.ds(base, HALF_D)], w.at[0], local_sem.at[0])
    own_w.start()
    kv[0, :, pl.ds(0, 256)] = k[...]
    kv[0, :, pl.ds(256, 256)] = v[...]

    yq = cp.go(own_q, w.at[4, quarter(0)], w_mate)
    xq = {0: (cp.go(own_q, w.at[3, quarter(0)], xp), cp.go(own_q, w.at[1, quarter(0)], xm))}
    ky = cp.go(kv.at[0], kv.at[4], kv_mate)
    kx = {0: (cp.go(kv.at[0], kv.at[3], xp), cp.go(kv.at[0], kv.at[1], xm))}
    yr = cp.go(own_r, w.at[4, rest], w_mate)
    xr = {0: (cp.go(own_r, w.at[3, rest], xp), cp.go(own_r, w.at[1, rest], xm))}
    swaps = [cp.go(gu, gu_oth, other), cp.go(dn, dn_oth, other)]
    zq, zq2 = {}, {}

    def z_first(slot):
        rows = quarter(0)
        zq[slot] = (
            cp.go(w.at[slot, rows], w.at[slot, rows], zp),
            cp.go(w.at[slot, rows], w.at[slot, rows], zm),
        )

    def z_second(slot):
        zq[slot][0].wait_recv()
        a = w.at[slot, quarter(3, 0)]
        zq[slot][1].wait_recv()
        b = w.at[slot, quarter(1, 1)]
        zq2[slot] = (cp.go(a, a, zp), cp.go(b, b, zm))

    def x_second(buf, d, firsts, parts):
        for c in firsts:
            c.wait_recv()
        return (
            cp.go(buf.at[4 * d + 3, parts[0]], buf.at[4 * d + 2, parts[0]], xp),
            cp.go(buf.at[4 * d + 1, parts[1]], buf.at[4 * d + 2, parts[1]], xm),
        )

    kv_parts = (pl.ds(0, 64), pl.ds(64, 64))
    q_parts = (quarter(0, 0), quarter(0, 1))
    yq.wait_recv()
    xq[1] = (
        cp.go(w.at[4, quarter(0)], w.at[7, quarter(0)], xp),
        cp.go(w.at[4, quarter(0)], w.at[5, quarter(0)], xm),
    )
    z_first(4)
    x2q = {0: x_second(w, 0, xq[0], q_parts)}
    z_first(3)
    z_first(1)
    ky.wait_recv()
    kx[1] = (cp.go(kv.at[4], kv.at[7], xp), cp.go(kv.at[4], kv.at[5], xm))
    kx2 = {0: x_second(kv, 0, kx[0], kv_parts)}
    x2q[1] = x_second(w, 1, xq[1], q_parts)
    z_first(7)
    z_first(5)
    kx2[1] = x_second(kv, 1, kx[1], kv_parts)
    for c in x2q[0]:
        c.wait_recv()
    z_first(2)
    for c in x2q[1]:
        c.wait_recv()
    z_first(6)
    z_second(4)
    yr.wait_recv()
    xr[1] = (cp.go(w.at[4, rest], w.at[7, rest], xp), cp.go(w.at[4, rest], w.at[5, rest], xm))
    for d in (0, 1):
        for c in kx2[d]:
            c.wait_recv()

    ctx = me["y_hi"] * 4 + me["x"]
    col = lax.broadcasted_iota(jnp.int32, (1, 1024), 1)
    key_pos = col % 64
    for slot in range(8):
        block = ((me["y_hi"] + slot // 4) % 2) * 4 + (me["x"] + slot % 4) % 4
        for h in (0, 1):
            key_pos = key_pos + jnp.where(
                col // 64 == 2 * slot + h, order[2 * block + h] * 64, 0
            )
    row = lax.broadcasted_iota(jnp.int32, (256, 1), 0) % TOK
    query_pos = row % 64 + jnp.where(row < 64, order[2 * ctx] * 64, order[2 * ctx + 1] * 64)
    bias = jnp.where(key_pos <= query_pos, 0.0, -1e30)

    def group(g):
        keys = kv[:, :, 64 * g : 64 * g + 64].reshape(1024, HEAD)
        values = kv[:, :, 256 + 64 * g : 256 + 64 * g + 64].reshape(1024, HEAD)

        def pair(i, _):
            lanes = pl.ds(pl.multiple_of((4 * g + i) * 128, 128), 128)
            two = q[:, lanes] * jnp.bfloat16(0.125)
            two = jnp.concatenate([two[:, :HEAD], two[:, HEAD:]], axis=0)
            s = lax.dot_general(
                two, keys, (((1,), (1,)), ((), ())), preferred_element_type=jnp.float32
            ) + bias
            p = jnp.exp(s - jnp.max(s, axis=1, keepdims=True))
            total = jnp.sum(p, axis=1, keepdims=True)
            o = jnp.dot(p.astype(jnp.bfloat16), values, preferred_element_type=jnp.float32)
            o = (o / total).astype(jnp.bfloat16)
            att[0, :, lanes] = jnp.concatenate([o[:TOK], o[TOK:]], axis=1)
            return 0

        lax.fori_loop(0, 4, pair, 0)

    group(0)
    z_second(3)
    z_second(1)
    x2r = {0: x_second(w, 0, xr[0], rest_parts)}
    group(1)
    z_second(7)
    z_second(5)
    group(2)
    x2r[1] = x_second(w, 1, xr[1], rest_parts)
    z_second(2)
    z_second(6)
    group(3)
    att_out = cp.go(att.at[0], att.at[1], other)
    own_w.wait()
    att_out.wait_recv()

    def project(slot, first=False):
        block = ((me["y_hi"] + slot // 4) % 2) * 4 + (me["x"] + slot % 4) % 4
        lanes = pl.ds(pl.multiple_of(block * 256, 256), 256)
        both = att[:, :, lanes].reshape(2 * TOK, 256)
        part = lax.dot_general(
            both, w[slot], (((1,), (1,)), ((), ())), preferred_element_type=jnp.float32
        ).reshape(2, TOK, HALF_D)
        acc[...] = part if first else acc[...] + part

    project(0, True)
    for slot in (4, 3, 1, 7, 5, 2, 6):
        d, s = slot // 4, slot % 4
        if slot == 4:
            pass
        elif s == 2:
            for c in x2r[d]:
                c.wait_recv()
        for c in zq2[slot]:
            c.wait_recv()
        project(slot)
    back = cp.go(acc.at[1], got, other)
    hidden = hid[...].astype(jnp.float32)
    back.wait_recv()
    mine, theirs = acc[0], got[...]
    left = jnp.where(core == 0, mine, theirs)
    right = jnp.where(core == 0, theirs, mine)
    res = (hidden + jnp.concatenate([left, right], axis=1)).astype(jnp.bfloat16)
    residual[...] = res
    res = res.astype(jnp.float32)
    scale = lax.rsqrt(jnp.mean(res * res, axis=1, keepdims=True) + 1e-05)
    moe_in[...] = (res * scale * gain[...]).astype(jnp.bfloat16)
    for c in swaps:
        c.wait_recv()
    cp.drain()


def front(q, k, v, hidden, gain, ow_t, order, gu_t, dn):
    vmem, anyspace = pl.BlockSpec(memory_space=pltpu.VMEM), pl.BlockSpec(memory_space=pl.ANY)
    bf = jnp.bfloat16
    return pl.pallas_call(
        front_kernel,
        out_shape=(
            jax.ShapeDtypeStruct((TOK, D), bf), jax.ShapeDtypeStruct((TOK, D), bf),
            jax.ShapeDtypeStruct(gu_t.shape, bf), jax.ShapeDtypeStruct(dn.shape, bf),
        ),
        in_specs=[pl.BlockSpec(memory_space=pltpu.SMEM), vmem, vmem, vmem, vmem, vmem, anyspace, anyspace, anyspace],
        out_specs=(vmem, vmem, anyspace, anyspace),
        scratch_shapes=[
            pltpu.VMEM((8, TOK, 512), bf),
            pltpu.VMEM((8, HALF_D, 256), bf),
            pltpu.VMEM((2, TOK, 2048), bf),
            pltpu.VMEM((2, TOK, HALF_D), jnp.float32),
            pltpu.VMEM((TOK, HALF_D), jnp.float32),
            pltpu.SemaphoreType.DMA((FRONT_COPIES,)),
            pltpu.SemaphoreType.DMA((FRONT_COPIES,)),
            pltpu.SemaphoreType.DMA((1,)),
        ],
        compiler_params=pltpu.CompilerParams(
            collective_id=0, has_side_effects=True, vmem_limit_bytes=48 * 2**20
        ),
    )(order, q, k, v, hidden, gain, ow_t, gu_t, dn)


PIECES = ((0, 1024), (1024, 1024), (2048, 832))
TURNS = (("x", "y", "z"), ("y", "z", "x"), ("z", "x", "y"))
ORDER = (0, 2, 1, 3)
MOE_COPIES = 200
STEP = 240


def moe_kernel(
    table, moe_in, residual, gu0, gu1, dn0, dn1,
    out, *refs,
):
    r2, q3, q2 = refs[0:3], refs[3:6], refs[6:9]
    t, s_buf, r3, tab, part, got = (refs[9 + 3 * i : 12 + 3 * i] for i in range(6))
    gu, dn, ffn, acc, send, recv, local_sem = refs[27:]
    me = here()
    cp = Copies(send, recv)
    near = []

    def copy(src, dst):
        c = pltpu.make_async_copy(src, dst, local_sem.at[len(near)])
        c.start()
        near.append(c)
        return c

    def go(src, dst, axis, by):
        if by == 0:
            return copy(src, dst)
        return cp.go(src, dst, moved(me, axis, by))

    def arrive(cs):
        for c in cs:
            if any(c is n for n in near):
                c.wait()
            else:
                c.wait_recv()

    greet([moved(me, a, by) for a in ("x", "y", "z") for by in (1, 3, 2)])
    loads = [copy(gu0, gu.at[0]), copy(gu1, gu.at[1]), copy(dn0, dn.at[0]), copy(dn1, dn.at[1])]

    tabs, ones, twos = {}, {}, {}
    for p in range(3):
        tab[p][0] = table[...]
        lo, width = PIECES[p]
        t[p][0] = moe_in[:, lo : lo + width]
    for p in range(3):
        a = TURNS[p][0]
        tabs[p] = [go(tab[p].at[0], tab[p].at[4 - by], a, by) for by in (1, 3, 2)]
    for p in range(3):
        a = TURNS[p][0]
        ones[p] = {3: go(t[p].at[0], t[p].at[3], a, 1), 1: go(t[p].at[0], t[p].at[1], a, 3)}
    halves = (pl.ds(0, 64), pl.ds(64, 64))
    for p in range(3):
        a = TURNS[p][0]
        ones[p][3].wait_recv()
        x = go(t[p].at[3, halves[0]], t[p].at[2, halves[0]], a, 1)
        ones[p][1].wait_recv()
        twos[p] = [x, go(t[p].at[1, halves[1]], t[p].at[2, halves[1]], a, 3)]

    row = lax.broadcasted_iota(jnp.int32, (256, 1), 0)
    y_me = me["y_hi"] * 2 + me["y_lo"]

    def row_code(p):
        at = {"x": me["x"], "y": y_me, "z": me["z"]}
        _, b, c = TURNS[p]
        at[b] = (at[b] + row // 64) % 4
        at[c] = (at[c] + (row // 16) % 4) % 4
        expert = (at["y"] // 2) * 32 + at["x"] * 8 + (at["y"] % 2) * 4 + at["z"]
        return (expert * 16 + row % 16).astype(jnp.float32)

    def rows_of(p, s):
        return s_buf[p].at[:, :, s] if p < 2 else s_buf[p].at[:, s]

    def build(p, s):
        code = row_code(p)
        width = PIECES[p][1]
        hit = tab[p][s, 0:1, :] == code
        for k in range(1, 4):
            hit = hit | (tab[p][s, k : k + 1, :] == code)
        pick = jnp.where(hit, 1.0, 0.0).astype(jnp.bfloat16)
        rows = jnp.dot(pick, t[p][s], preferred_element_type=jnp.float32).astype(jnp.bfloat16)
        rows_of(p, s)[...] = rows.reshape(4, 4, 16, width)

    for p in range(3):
        for c in tabs[p]:
            c.wait_recv()
        for s in (0, 3, 1):
            build(p, s)
    for p in range(3):
        for c in twos[p]:
            c.wait_recv()
        build(p, 2)

    second = {d: [] for d in ORDER}
    for d in ORDER:
        c = (4 - d) % 4
        for b in (1, 3, 2):
            o = 4 - b
            second[d].append(go(s_buf[0].at[b, c], r2[0].at[o, c], "y", b))
            second[d].append(go(s_buf[2].at[b, d], r2[2].at[o, d], "x", b))
        if d:
            second[d].append(go(s_buf[1].at[4 - d], r2[1].at[d], "z", 4 - d))

    third = {}

    def forward(d):
        arrive(second[d])
        cs = []
        c0 = (4 - d) % 4
        cs.append(go(r2[0].at[pl.ds(1, 3), c0], r3[0].at[d, pl.ds(1, 3)], "z", c0))
        cs.append(go(s_buf[0].at[0, c0], r3[0].at[d, 0], "z", c0))
        for c in (1, 3, 2, 0):
            o = (4 - c) % 4
            src = r2[1].at[d, c] if d else s_buf[1].at[0, c]
            cs.append(go(src, r3[1].at[d, :, o], "x", c))
            cs.append(go(r2[2].at[pl.ds(1, 3), d, c], r3[2].at[d, o, pl.ds(1, 3)], "y", c))
            cs.append(go(s_buf[2].at[0, d, c], r3[2].at[d, o, 0], "y", c))
        third[d] = cs

    def experts(d):
        arrive(third[d])
        xs = [r3[p][d].reshape(256, PIECES[p][1]) for p in range(3)]

        def step(i, _):
            h = i // 3
            at = (i % 3) * STEP

            def side(start):
                total = None
                for p in range(3):
                    lo, width = PIECES[p]
                    w = gu[h, pl.ds(pl.multiple_of(start, 16), STEP), lo : lo + width]
                    y = lax.dot_general(
                        xs[p], w, (((1,), (1,)), ((), ())), preferred_element_type=jnp.float32
                    )
                    total = y if total is None else total + y
                return total

            gate, up = side(at), side(D // 4 + at)
            act = (gate * (1.0 / (1.0 + jnp.exp(-1.702 * gate))) * (up + 1.0)).astype(jnp.bfloat16)
            w = dn[h, pl.ds(pl.multiple_of(at, 16), STEP), :]
            y = jnp.dot(act, w, preferred_element_type=jnp.float32)

            @pl.when(i == 0)
            def _():
                ffn[...] = y

            @pl.when(i > 0)
            def _():
                ffn[...] += y

            return 0

        lax.fori_loop(0, 6, step, 0)
        for p in range(3):
            lo, width = PIECES[p]
            r3[p][d] = ffn[:, lo : lo + width].astype(jnp.bfloat16).reshape(4, 4, 16, width)

    back3, back2 = {}, {}

    def give_back(d):
        cs, done = [], []
        c0 = (4 - d) % 4
        if d:
            cs.append(go(r3[0].at[d, pl.ds(1, 3)], q3[0].at[pl.ds(1, 3), c0], "z", d))
        done.append(go(r3[0].at[d, 0], q2[0].at[0, c0], "z", d))
        for o in (1, 3, 2, 0):
            c = (4 - o) % 4
            if d == 0:
                done.append(go(r3[1].at[d, :, o], q2[1].at[0, c], "x", o))
            elif o:
                cs.append(go(r3[1].at[d, :, o], q3[1].at[d, c], "x", o))
            if o:
                cs.append(go(r3[2].at[d, o, pl.ds(1, 3)], q3[2].at[pl.ds(1, 3), d, c], "y", o))
            done.append(go(r3[2].at[d, o, 0], q2[2].at[0, d, c], "y", o))
        back3[d] = cs
        back2[d] = done

    def hand_on(d):
        arrive(back3[d])
        cs = back2[d]
        c0 = (4 - d) % 4
        for o in (1, 3, 2):
            b = 4 - o
            src = q3[0].at[o, c0] if d else r3[0].at[0, o]
            cs.append(go(src, q2[0].at[b, c0], "y", o))
            cs.append(go(r3[2].at[d, 0, o], q2[2].at[b, d, 0], "x", o))
            cs.append(go(q3[2].at[o, d, pl.ds(1, 3)], q2[2].at[b, d, pl.ds(1, 3)], "x", o))
        if d:
            cs.append(go(r3[1].at[d, :, 0], q2[1].at[4 - d, 0], "z", d))
            cs.append(go(q3[1].at[d, pl.ds(1, 3)], q2[1].at[4 - d, pl.ds(1, 3)], "z", d))

    forward(0)
    forward(2)
    for c in loads:
        c.wait()
    experts(0)
    give_back(0)
    forward(1)
    forward(3)
    experts(2)
    give_back(2)
    hand_on(0)
    experts(1)
    give_back(1)
    hand_on(2)
    experts(3)
    give_back(3)
    hand_on(1)
    hand_on(3)
    for d in ORDER:
        arrive(back2[d])
    cp.drain()
    fetch = [copy(q2[p], s_buf[p]) for p in range(3)]
    for c in fetch:
        c.wait()

    last = []

    def combine(p, s):
        code = row_code(p)
        width = PIECES[p][1]
        spread = jnp.zeros((256, TOK), jnp.float32)
        for k in range(4):
            spread = spread + jnp.where(
                tab[p][s, k : k + 1, :] == code, tab[p][s, 4 + k : 5 + k, :], 0.0
            )
        high = spread.astype(jnp.bfloat16)
        low = (spread - high.astype(jnp.float32)).astype(jnp.bfloat16)
        rows = rows_of(p, s)[...].reshape(256, width)
        over = (((0,), (0,)), ((), ()))
        return lax.dot_general(
            high, rows, over, preferred_element_type=jnp.float32
        ) + lax.dot_general(low, rows, over, preferred_element_type=jnp.float32)

    for s in (1, 3, 2):
        for p in range(3):
            part[p][s - 1] = combine(p, s).astype(jnp.bfloat16)
            last.append(go(part[p].at[s - 1], got[p].at[3 - s], TURNS[p][0], s))
    for p in range(3):
        lo, width = PIECES[p]
        acc[:, lo : lo + width] = residual[:, lo : lo + width].astype(jnp.float32) + combine(p, 0)
    for c in last:
        c.wait_recv()
    for p in range(3):
        lo, width = PIECES[p]
        total = acc[:, lo : lo + width]
        for i in range(3):
            total = total + got[p][i].astype(jnp.float32)
        out[:, lo : lo + width] = total.astype(jnp.bfloat16)
    for c in last:
        c.wait_send()


def moe(table, moe_in, residual, gu0, gu1, dn0, dn1):
    vmem, anyspace = pl.BlockSpec(memory_space=pltpu.VMEM), pl.BlockSpec(memory_space=pl.ANY)
    bf = jnp.bfloat16
    widths = [w for _, w in PIECES]
    far = [jax.ShapeDtypeStruct((4, 4, 4, 16, w), bf) for w in widths] * 3
    return pl.pallas_call(
        moe_kernel,
        out_shape=(jax.ShapeDtypeStruct((TOK, D), bf), *far),
        in_specs=[vmem] * 3 + [anyspace] * 4,
        out_specs=(vmem, *([anyspace] * 9)),
        scratch_shapes=[
            *(pltpu.VMEM((4, TOK, w), bf) for w in widths),
            *(pltpu.VMEM((4, 4, 4, 16, w), bf) for w in widths),
            *(pltpu.VMEM((4, 4, 4, 16, w), bf) for w in widths),
            *(pltpu.VMEM((4, 8, TOK), jnp.float32) for w in widths),
            *(pltpu.VMEM((3, TOK, w), bf) for w in widths),
            *(pltpu.VMEM((3, TOK, w), bf) for w in widths),
            pltpu.VMEM((2, HALF_D, D), bf),
            pltpu.VMEM((2, HALF_D // 2, D), bf),
            pltpu.VMEM((256, D), jnp.float32),
            pltpu.VMEM((TOK, D), jnp.float32),
            pltpu.SemaphoreType.DMA((MOE_COPIES,)),
            pltpu.SemaphoreType.DMA((MOE_COPIES,)),
            pltpu.SemaphoreType.DMA((64,)),
        ],
        compiler_params=pltpu.CompilerParams(
            collective_id=1, has_side_effects=True, vmem_limit_bytes=60 * 2**20
        ),
    )(table, moe_in, residual, gu0, gu1, dn0, dn1)[0]


def route_table(ids, weights):
    named = ids[:, :, None] == jnp.arange(64, dtype=jnp.int32)
    member = jnp.any(named, axis=1).astype(jnp.bfloat16)
    tok = jnp.arange(TOK, dtype=jnp.int32)
    before = (tok[None, :] < tok[:, None]).astype(jnp.bfloat16)
    slot = jnp.dot(before, member, preferred_element_type=jnp.float32)
    slot_of = jnp.sum(jnp.where(named, slot[:, None, :], 0.0), axis=2)
    code = ids.astype(jnp.float32) * 16.0 + slot_of
    return jnp.concatenate([code, weights], axis=1).T


def local(
    queries, key_rows, value_matrix, hidden, out_weight, norm_gain, block_order,
    expert_ids, route_weights, gate_up_weight, down_weight,
):
    gate_up_own, down_own = gate_up_weight[0].T, down_weight[0]
    table = route_table(expert_ids[0], route_weights[0])
    residual, moe_in, gate_up_oth, down_oth = front(
        queries[0], key_rows[0], value_matrix[0], hidden[0], norm_gain[None], out_weight.T,
        block_order, gate_up_own, down_own,
    )
    return moe(table, moe_in, residual, gate_up_own, gate_up_oth, down_own, down_oth)[None]


def solution(mesh):
    fine = Mesh(mesh.devices.reshape(2, 4, 2, 4, 2), ("y_hi", "x", "y_lo", "z", "core"))
    rows = P(EXP, CTX, None)
    halves = P(CTX + EXP, None, None)
    return jax.shard_map(
        local,
        mesh=fine,
        in_specs=(
            rows, rows, rows, rows, P(CTX, None), P(), P(), rows, rows, halves, halves,
        ),
        out_specs=rows,
        check_vma=False,
    )
```

```python
import functools
import jax
import jax.numpy as jnp
from jax import lax
from jax.experimental import pallas as pl
from jax.experimental.pallas import tpu as pltpu
from jax.sharding import Mesh, PartitionSpec as P

D = 2880
HALF_D = D // 2
HEAD = 64
TOK = 128
QUARTER = 240
Q_FIRST = 128
REST = HALF_D - 4 * QUARTER
AXES = ("y_hi", "x", "y_lo", "z", "core")
MESH = pl.DeviceIdType.MESH
PIECES = ((0, 1024), (1024, 1024), (2048, 832))
CTX = ("y_hi", "x")
EXP = ("y_lo", "z", "core")


def here():
    return {a: lax.axis_index(a) for a in AXES}


def moved(me, axis, by):
    to = dict(me)
    if axis == "y":
        y = (me["y_hi"] * 2 + me["y_lo"] + by) % 4
        to["y_hi"], to["y_lo"] = y // 2, y % 2
    else:
        to[axis] = (me[axis] + by) % 4
    return to


class Copies:
    def __init__(self, send, recv):
        self.send, self.recv, self.made = send, recv, []

    def go(self, src, dst, to):
        i = len(self.made)
        c = pltpu.make_async_remote_copy(
            src_ref=src, dst_ref=dst, send_sem=self.send.at[i], recv_sem=self.recv.at[i],
            device_id=to, device_id_type=MESH,
        )
        c.start()
        self.made.append(c)
        return c

    def drain(self):
        for c in self.made:
            c.wait_send()


def greet(peers):
    barrier = pltpu.get_barrier_semaphore()
    for peer in peers:
        pl.semaphore_signal(barrier, inc=1, device_id=peer, device_id_type=MESH)
    pl.semaphore_wait(barrier, len(peers))


FRONT_COPIES = 80


def front_kernel(
    order, q_in, k_in, v_in, hid_in, gain_in, ow, ids_in, weights_in, gu, dn,
    residual, moe0, moe1, moe2, table, gu_oth, dn_oth,
    q, hid, gain, ids, kv, w, att, acc, got, rows, res_out, m0, m1, m2, tab, send, recv, local_sem,
):
    me = here()
    cp = Copies(send, recv)
    near = []

    def copy(src, dst):
        c = pltpu.make_async_copy(src, dst, local_sem.at[len(near)])
        c.start()
        near.append(c)
        return c

    core = me["core"]
    base = pl.multiple_of(core * HALF_D, 16)
    kv_in = (copy(k_in, kv.at[0, :, pl.ds(0, 256)]), copy(v_in, kv.at[0, :, pl.ds(256, 256)]))
    q_copy = copy(q_in, q)
    ids_copy, weights_copy = copy(ids_in, ids), copy(weights_in, tab.at[pl.ds(4, 4)])
    hid_copy, gain_copy = copy(hid_in, hid), copy(gain_in, gain)
    own_w = copy(ow.at[pl.ds(base, HALF_D)], w.at[0])

    other = dict(me, core=1 - core)
    kv_mate = dict(me, y_hi=1 - me["y_hi"])
    w_mate = dict(me, y_hi=1 - me["y_hi"], y_lo=1 - me["y_lo"])
    xp, xm = moved(me, "x", 1), moved(me, "x", 3)
    zp, zm = moved(me, "z", 1), moved(me, "z", 3)
    z = me["z"]
    greet([other, kv_mate, w_mate, xp, xm, zp, zm])

    def quarter(t, part=None):
        start = REST + QUARTER * ((z + t) % 4)
        size = QUARTER
        if part == 0:
            size = Q_FIRST
        elif part == 1:
            start, size = start + Q_FIRST, QUARTER - Q_FIRST
        return pl.ds(pl.multiple_of(start, 16), size)

    own_q = ow.at[pl.ds(pl.multiple_of(base + REST + QUARTER * z, 16), QUARTER)]
    own_r = ow.at[pl.ds(base, REST)]
    rest = pl.ds(0, REST)
    rest_parts = (pl.ds(0, REST // 2), pl.ds(REST // 2, REST // 2))
    kv_parts = (pl.ds(0, 64), pl.ds(64, 64))
    q_parts = (quarter(0, 0), quarter(0, 1))
    zq, zq2 = {}, {}

    def z_first(slot):
        part = w.at[slot, quarter(0)]
        zq[slot] = (cp.go(part, part, zp), cp.go(part, part, zm))

    def z_second(slot):
        for c in zq[slot]:
            c.wait_recv()
        a, b = w.at[slot, quarter(3, 0)], w.at[slot, quarter(1, 1)]
        zq2[slot] = (cp.go(a, a, zp), cp.go(b, b, zm))

    def x_first(buf, slot, part):
        src = buf.at[slot, part]
        return cp.go(src, buf.at[slot + 3, part], xp), cp.go(src, buf.at[slot + 1, part], xm)

    def x_second(buf, d, firsts, parts):
        for c in firsts:
            c.wait_recv()
        return (
            cp.go(buf.at[4 * d + 3, parts[0]], buf.at[4 * d + 2, parts[0]], xp),
            cp.go(buf.at[4 * d + 1, parts[1]], buf.at[4 * d + 2, parts[1]], xm),
        )

    def arrive(cs):
        for c in cs:
            c.wait_recv()

    yq = cp.go(own_q, w.at[4, quarter(0)], w_mate)
    xq0 = (cp.go(own_q, w.at[3, quarter(0)], xp), cp.go(own_q, w.at[1, quarter(0)], xm))
    for c in kv_in:
        c.wait()
    ky = cp.go(kv.at[0], kv.at[4], kv_mate)
    swaps = [cp.go(gu, gu_oth, other), cp.go(dn, dn_oth, other)]
    yq.wait_recv()
    xq1 = x_first(w, 4, quarter(0))
    z_first(4)
    every = pl.ds(0, TOK)
    kx0 = x_first(kv, 0, every)
    x2q0 = x_second(w, 0, xq0, q_parts)
    z_first(3)
    z_first(1)
    ky.wait_recv()
    kx1 = x_first(kv, 4, every)
    x2q1 = x_second(w, 1, xq1, q_parts)
    z_first(7)
    z_first(5)
    kx20 = x_second(kv, 0, kx0, kv_parts)
    yr = [cp.go(own_r, w.at[4, rest], w_mate)]
    xr = (cp.go(own_r, w.at[3, rest], xp), cp.go(own_r, w.at[1, rest], xm))
    arrive(x2q0)
    z_first(2)
    kx21 = x_second(kv, 1, kx1, kv_parts)
    arrive(x2q1)
    z_first(6)
    z_second(4)

    ids_copy.wait()
    weights_copy.wait()
    expert = lax.broadcasted_iota(jnp.int32, (64, TOK), 0)
    hits = [ids[k : k + 1, :] == expert for k in range(4)]
    member = jnp.where(hits[0] | hits[1] | hits[2] | hits[3], 1.0, 0.0).astype(jnp.bfloat16)
    earlier = jnp.where(
        lax.broadcasted_iota(jnp.int32, (TOK, TOK), 0) < lax.broadcasted_iota(jnp.int32, (TOK, TOK), 1),
        1.0, 0.0,
    ).astype(jnp.bfloat16)
    place = jnp.dot(member, earlier, preferred_element_type=jnp.float32)
    for k in range(4):
        slot_of = jnp.sum(jnp.where(hits[k], place, 0.0), axis=0, keepdims=True)
        tab[k : k + 1, :] = ids[k : k + 1, :].astype(jnp.float32) * 16.0 + slot_of
    tab_out = copy(tab, table)

    hid_copy.wait()
    for lo in range(0, D, 128):
        n = min(128, D - lo)
        rows[:, lo : lo + n] = hid[lo : lo + n, :].astype(jnp.float32).T

    ctx = me["y_hi"] * 4 + me["x"]
    col = lax.broadcasted_iota(jnp.int32, (1, 1024), 1)
    key_pos = col % 64
    for slot in range(8):
        block = ((me["y_hi"] + slot // 4) % 2) * 4 + (me["x"] + slot % 4) % 4
        for h in (0, 1):
            key_pos = key_pos + jnp.where(
                col // 64 == 2 * slot + h, order[2 * block + h] * 64, 0
            )
    row = lax.broadcasted_iota(jnp.int32, (256, 1), 0) % TOK
    query_pos = row % 64 + jnp.where(row < 64, order[2 * ctx] * 64, order[2 * ctx + 1] * 64)
    bias = jnp.where(key_pos <= query_pos, 0.0, -1e30)
    q_copy.wait()
    arrive(kx20)
    arrive(kx21)

    def group(g):
        keys = kv[:, :, 64 * g : 64 * g + 64].reshape(1024, HEAD)
        values = kv[:, :, 256 + 64 * g : 256 + 64 * g + 64].reshape(1024, HEAD)

        def pair(i, _):
            lanes = pl.ds(pl.multiple_of((4 * g + i) * 128, 128), 128)
            two = q[:, lanes] * jnp.bfloat16(0.125)
            two = jnp.concatenate([two[:, :HEAD], two[:, HEAD:]], axis=0)
            s = lax.dot_general(
                two, keys, (((1,), (1,)), ((), ())), preferred_element_type=jnp.float32
            ) + bias
            p = jnp.exp(s - jnp.max(s, axis=1, keepdims=True))
            total = jnp.sum(p, axis=1, keepdims=True)
            o = jnp.dot(p.astype(jnp.bfloat16), values, preferred_element_type=jnp.float32)
            o = (o / total).astype(jnp.bfloat16)
            att[0, :, lanes] = jnp.concatenate([o[:TOK], o[TOK:]], axis=1)
            return 0

        lax.fori_loop(0, 4, pair, 0)

    group(0)
    z_second(3)
    z_second(1)
    x2r = x_second(w, 0, xr, rest_parts)
    yr.append(cp.go(w.at[3, rest], w.at[7, rest], w_mate))
    yr.append(cp.go(w.at[1, rest], w.at[5, rest], w_mate))
    group(1)
    z_second(7)
    z_second(5)
    arrive(x2r)
    yr.append(cp.go(w.at[2, rest], w.at[6, rest], w_mate))
    group(2)
    z_second(2)
    z_second(6)
    group(3)
    att_out = cp.go(att.at[0], att.at[1], other)
    own_w.wait()
    att_out.wait_recv()

    def project(slot, first=False):
        block = ((me["y_hi"] + slot // 4) % 2) * 4 + (me["x"] + slot % 4) % 4
        lanes = pl.ds(pl.multiple_of(block * 256, 256), 256)
        both = att[:, :, lanes].reshape(2 * TOK, 256)
        part = lax.dot_general(
            both, w[slot], (((1,), (1,)), ((), ())), preferred_element_type=jnp.float32
        ).reshape(2, TOK, HALF_D)
        acc[...] = part if first else acc[...] + part

    project(0, True)
    for slot in (3, 1, 4, 7, 5, 2, 6):
        arrive(zq2[slot])
        if slot >= 4:
            yr[{4: 0, 7: 1, 5: 2, 6: 3}[slot]].wait_recv()
        project(slot)
    back = cp.go(acc.at[1], got, other)
    gain_copy.wait()
    back.wait_recv()
    mine, theirs = acc[0], got[...]
    left = jnp.where(core == 0, mine, theirs)
    right = jnp.where(core == 0, theirs, mine)
    res = (rows[...] + jnp.concatenate([left, right], axis=1)).astype(jnp.bfloat16)
    res_out[...] = res
    outs = [copy(res_out, residual)]
    res = res.astype(jnp.float32)
    scale = lax.rsqrt(jnp.mean(res * res, axis=1, keepdims=True) + 1e-05)
    normed = (res * scale * gain[...].reshape(1, D)).astype(jnp.bfloat16)
    for (lo, width), m, o in zip(PIECES, (m0, m1, m2), (moe0, moe1, moe2), strict=True):
        m[...] = normed[:, lo : lo + width]
        outs.append(copy(m, o))
    for c in outs:
        c.wait()
    tab_out.wait()
    arrive(swaps)
    cp.drain()


def front(q, k, v, hidden_t, gain, ow_t, order, ids_t, weights_t, gu_t, dn):
    anyspace = pl.BlockSpec(memory_space=pl.ANY)
    bf = jnp.bfloat16
    pieces = [(TOK, width) for _, width in PIECES]
    return pl.pallas_call(
        front_kernel,
        out_shape=(
            jax.ShapeDtypeStruct((TOK, D), bf),
            *(jax.ShapeDtypeStruct(p, bf) for p in pieces),
            jax.ShapeDtypeStruct((8, TOK), jnp.float32),
            jax.ShapeDtypeStruct(gu_t.shape, bf), jax.ShapeDtypeStruct(dn.shape, bf),
        ),
        in_specs=[pl.BlockSpec(memory_space=pltpu.SMEM)] + [anyspace] * 10,
        out_specs=(anyspace,) * 7,
        scratch_shapes=[
            pltpu.VMEM((TOK, 2048), bf),
            pltpu.VMEM((D, TOK), bf),
            pltpu.VMEM((D,), jnp.float32),
            pltpu.VMEM((4, TOK), jnp.int32),
            pltpu.VMEM((8, TOK, 512), bf),
            pltpu.VMEM((8, HALF_D, 256), bf),
            pltpu.VMEM((2, TOK, 2048), bf),
            pltpu.VMEM((2, TOK, HALF_D), jnp.float32),
            pltpu.VMEM((TOK, HALF_D), jnp.float32),
            pltpu.VMEM((TOK, D), jnp.float32),
            pltpu.VMEM((TOK, D), bf),
            *(pltpu.VMEM(p, bf) for p in pieces),
            pltpu.VMEM((8, TOK), jnp.float32),
            pltpu.SemaphoreType.DMA((FRONT_COPIES,)),
            pltpu.SemaphoreType.DMA((FRONT_COPIES,)),
            pltpu.SemaphoreType.DMA((16,)),
        ],
        compiler_params=pltpu.CompilerParams(
            collective_id=0, has_side_effects=True, vmem_limit_bytes=60 * 2**20
        ),
    )(order, q, k, v, hidden_t, gain, ow_t, ids_t, weights_t, gu_t, dn)


TURNS = (("x", "y", "z"), ("y", "z", "x"), ("z", "x", "y"))
ORDER = (0, 2, 1, 3)
MOE_COPIES = 200
FF_HALF = 720


def moe_kernel(
    table, in0, in1, in2, residual, gu0, gu1, dn0, dn1,
    out, *refs,
):
    r2, q3 = refs[0:3], refs[3:6]
    t, s_buf, r3, q2, tab, part, got = (refs[6 + 3 * i : 9 + 3 * i] for i in range(7))
    gu, dn, act, res, send, recv, local_sem = refs[27:]
    me = here()
    cp = Copies(send, recv)
    near = []

    def copy(src, dst):
        c = pltpu.make_async_copy(src, dst, local_sem.at[len(near)])
        c.start()
        near.append(c)
        return c

    def go(src, dst, axis, by):
        if by == 0:
            return copy(src, dst)
        return cp.go(src, dst, moved(me, axis, by))

    def arrive(cs):
        for c in cs:
            if any(c is n for n in near):
                c.wait()
            else:
                c.wait_recv()

    tab_in = [copy(table, tab[p].at[0]) for p in range(3)]
    own_in = [copy(src, t[p].at[0]) for p, src in enumerate((in0, in1, in2))]
    loads = [copy(gu0, gu.at[0]), copy(gu1, gu.at[1]), copy(dn0, dn.at[0]), copy(dn1, dn.at[1])]
    res_in = copy(residual, res)
    greet([moved(me, a, by) for a in ("x", "y", "z") for by in (1, 3, 2)])

    tabs, ones, twos = {}, {}, {}
    for p in range(3):
        a = TURNS[p][0]
        tab_in[p].wait()
        tabs[p] = [go(tab[p].at[0], tab[p].at[4 - by], a, by) for by in (1, 3, 2)]
    for p in range(3):
        a = TURNS[p][0]
        own_in[p].wait()
        ones[p] = (go(t[p].at[0], t[p].at[3], a, 1), go(t[p].at[0], t[p].at[1], a, 3))

    row = lax.broadcasted_iota(jnp.int32, (256, 1), 0)
    y_me = me["y_hi"] * 2 + me["y_lo"]

    def row_code(p):
        at = {"x": me["x"], "y": y_me, "z": me["z"]}
        _, b, c = TURNS[p]
        at[b] = (at[b] + row // 64) % 4
        at[c] = (at[c] + (row // 16) % 4) % 4
        expert = (at["y"] // 2) * 32 + at["x"] * 8 + (at["y"] % 2) * 4 + at["z"]
        return (expert * 16 + row % 16).astype(jnp.float32)

    def rows_of(bufs, p, s):
        return bufs[p].at[:, :, s] if p < 2 else bufs[p].at[:, s]

    def build(p, s):
        code = row_code(p)
        width = PIECES[p][1]
        hit = tab[p][s, 0:1, :] == code
        for k in range(1, 4):
            hit = hit | (tab[p][s, k : k + 1, :] == code)
        pick = jnp.where(hit, 1.0, 0.0).astype(jnp.bfloat16)
        rows = jnp.dot(pick, t[p][s], preferred_element_type=jnp.float32).astype(jnp.bfloat16)
        rows_of(s_buf, p, s)[...] = rows.reshape(4, 4, 16, width)

    second = {d: [] for d in ORDER}

    def second_two(d):
        for b in (1, 3, 2):
            second[d].append(go(s_buf[2].at[b, d], r2[2].at[4 - b, d], "x", b))

    build(2, 0)
    second_two(0)
    build(0, 0)
    build(1, 0)
    halves = (pl.ds(0, 64), pl.ds(64, 64))
    for p in range(3):
        a = TURNS[p][0]
        arrive(ones[p])
        twos[p] = (
            go(t[p].at[3, halves[0]], t[p].at[2, halves[0]], a, 1),
            go(t[p].at[1, halves[1]], t[p].at[2, halves[1]], a, 3),
        )
    for p in (2, 0, 1):
        arrive(tabs[p])
        for s in (3, 1):
            build(p, s)
    for p in (0, 1, 2):
        arrive(twos[p])
        build(p, 2)
    for d in ORDER:
        c = (4 - d) % 4
        for b in (1, 3, 2):
            second[d].append(go(s_buf[0].at[b, c], r2[0].at[4 - b, c], "y", b))
        if d:
            second_two(d)
            second[d].append(go(s_buf[1].at[4 - d], r2[1].at[d], "z", 4 - d))

    third = {}

    def forward(d):
        arrive(second[d])
        cs = []
        c0 = (4 - d) % 4
        cs.append(go(r2[0].at[pl.ds(1, 3), c0], r3[0].at[d, pl.ds(1, 3)], "z", c0))
        cs.append(go(s_buf[0].at[0, c0], r3[0].at[d, 0], "z", c0))
        for c in (1, 3, 2, 0):
            o = (4 - c) % 4
            src = r2[1].at[d, c] if d else s_buf[1].at[0, c]
            cs.append(go(src, r3[1].at[d, :, o], "x", c))
            cs.append(go(r2[2].at[pl.ds(1, 3), d, c], r3[2].at[d, o, pl.ds(1, 3)], "y", c))
            cs.append(go(s_buf[2].at[0, d, c], r3[2].at[d, o, 0], "y", c))
        third[d] = cs

    back3, back2 = {}, {}

    def give_back(d, p):
        cs, done = [], []
        c0 = (4 - d) % 4
        if p == 0:
            if d:
                cs.append(go(r3[0].at[d, pl.ds(1, 3)], q3[0].at[pl.ds(1, 3), c0], "z", d))
            done.append(go(r3[0].at[d, 0], q2[0].at[0, c0], "z", d))
        for o in (1, 3, 2, 0):
            c = (4 - o) % 4
            if p == 1:
                if d == 0:
                    done.append(go(r3[1].at[d, :, o], q2[1].at[0, c], "x", o))
                elif o:
                    cs.append(go(r3[1].at[d, :, o], q3[1].at[d, c], "x", o))
            elif p == 2:
                if o:
                    cs.append(go(r3[2].at[d, o, pl.ds(1, 3)], q3[2].at[pl.ds(1, 3), d, c], "y", o))
                done.append(go(r3[2].at[d, o, 0], q2[2].at[0, d, c], "y", o))
        back3[p, d] = cs
        back2[p, d] = done

    def hand_on(d):
        c0 = (4 - d) % 4
        arrive(back3[0, d])
        for o in (1, 3, 2):
            src = q3[0].at[o, c0] if d else r3[0].at[0, o]
            back2[0, d].append(go(src, q2[0].at[4 - o, c0], "y", o))
        arrive(back3[1, d])
        if d:
            back2[1, d].append(go(r3[1].at[d, :, 0], q2[1].at[4 - d, 0], "z", d))
            back2[1, d].append(
                go(q3[1].at[d, pl.ds(1, 3)], q2[1].at[4 - d, pl.ds(1, 3)], "z", d)
            )
        arrive(back3[2, d])
        for o in (1, 3, 2):
            b = 4 - o
            back2[2, d].append(go(r3[2].at[d, 0, o], q2[2].at[b, d, 0], "x", o))
            back2[2, d].append(
                go(q3[2].at[o, d, pl.ds(1, 3)], q2[2].at[b, d, pl.ds(1, 3)], "x", o)
            )

    def experts(d, between):
        arrive(third[d])
        xs = [r3[p][d].reshape(256, PIECES[p][1]) for p in range(3)]

        def first(h, _):
            def side(start):
                total = None
                for p in range(3):
                    lo, width = PIECES[p]
                    y = lax.dot_general(
                        xs[p], gu[h, start : start + FF_HALF, lo : lo + width],
                        (((1,), (1,)), ((), ())), preferred_element_type=jnp.float32,
                    )
                    total = y if total is None else total + y
                return total

            gate, up = side(0), side(FF_HALF)
            act[h] = (gate * (1.0 / (1.0 + jnp.exp(-1.702 * gate))) * (up + 1.0)).astype(jnp.bfloat16)
            return 0

        lax.fori_loop(0, 2, first, 0)
        between()
        for p in range(3):
            lo, width = PIECES[p]
            y = jnp.dot(
                act[0], dn[0, :, lo : lo + width], preferred_element_type=jnp.float32
            ) + jnp.dot(act[1], dn[1, :, lo : lo + width], preferred_element_type=jnp.float32)
            r3[p][d] = y.astype(jnp.bfloat16).reshape(4, 4, 16, width)
            give_back(d, p)

    last = []

    def combine(p, s):
        code = row_code(p)
        width = PIECES[p][1]
        spread = jnp.zeros((256, TOK), jnp.float32)
        for k in range(4):
            spread = spread + jnp.where(
                tab[p][s, k : k + 1, :] == code, tab[p][s, 4 + k : 5 + k, :], 0.0
            )
        high = spread.astype(jnp.bfloat16)
        low = (spread - high.astype(jnp.float32)).astype(jnp.bfloat16)
        rows = rows_of(q2, p, s)[...].reshape(256, width)
        over = (((0,), (0,)), ((), ()))
        return lax.dot_general(
            high, rows, over, preferred_element_type=jnp.float32
        ) + lax.dot_general(low, rows, over, preferred_element_type=jnp.float32)

    def hand_in(p, s):
        part[p][s - 1] = combine(p, s).astype(jnp.bfloat16)
        last.append(go(part[p].at[s - 1], got[p].at[3 - s], TURNS[p][0], s))

    forward(0)
    forward(2)
    for c in loads:
        c.wait()
    experts(0, lambda: forward(1))
    experts(2, lambda: (forward(3), hand_on(0)))
    experts(1, lambda: hand_on(2))
    experts(3, lambda: hand_on(1))
    arrive(back2[2, 2])
    hand_in(2, 2)
    hand_on(3)
    arrive(back2[2, 1])
    hand_in(2, 1)
    for p in (0, 1):
        for d in ORDER:
            arrive(back2[p, d])
        for s in (1, 3, 2):
            hand_in(p, s)
    arrive(back2[2, 3])
    hand_in(2, 3)
    arrive(back2[2, 0])
    res_in.wait()
    owns = []
    for p in range(3):
        lo, width = PIECES[p]
        owns.append(res[:, lo : lo + width].astype(jnp.float32) + combine(p, 0))
    for c in last:
        c.wait_recv()
    for p in range(3):
        lo, width = PIECES[p]
        total = owns[p]
        for i in range(3):
            total = total + got[p][i].astype(jnp.float32)
        for at in range(0, width, 128):
            n = min(128, width - at)
            out[lo + at : lo + at + n, :] = total[:, at : at + n].T.astype(jnp.bfloat16)
    cp.drain()


def moe(table, pieces, residual, gu0, gu1, dn0, dn1):
    vmem, anyspace = pl.BlockSpec(memory_space=pltpu.VMEM), pl.BlockSpec(memory_space=pl.ANY)
    bf = jnp.bfloat16
    widths = [w for _, w in PIECES]
    far = [jax.ShapeDtypeStruct((4, 4, 4, 16, w), bf) for w in widths] * 2
    return pl.pallas_call(
        moe_kernel,
        out_shape=(jax.ShapeDtypeStruct((D, TOK), bf), *far),
        in_specs=[anyspace] * 9,
        out_specs=(vmem, *([anyspace] * 6)),
        scratch_shapes=[
            *(pltpu.VMEM((4, TOK, w), bf) for w in widths),
            *(pltpu.VMEM((4, 4, 4, 16, w), bf) for w in widths * 3),
            *(pltpu.VMEM((4, 8, TOK), jnp.float32) for w in widths),
            *(pltpu.VMEM((3, TOK, w), bf) for w in widths),
            *(pltpu.VMEM((3, TOK, w), bf) for w in widths),
            pltpu.VMEM((2, HALF_D, D), bf),
            pltpu.VMEM((2, FF_HALF, D), bf),
            pltpu.VMEM((2, 256, FF_HALF), bf),
            pltpu.VMEM((TOK, D), bf),
            pltpu.SemaphoreType.DMA((MOE_COPIES,)),
            pltpu.SemaphoreType.DMA((MOE_COPIES,)),
            pltpu.SemaphoreType.DMA((64,)),
        ],
        compiler_params=pltpu.CompilerParams(
            collective_id=1, has_side_effects=True, vmem_limit_bytes=60 * 2**20
        ),
    )(table, *pieces, residual, gu0, gu1, dn0, dn1)[0]


def local(
    queries, key_rows, value_matrix, hidden, out_weight, norm_gain, block_order,
    expert_ids, route_weights, gate_up_weight, down_weight,
):
    gate_up_own, down_own = gate_up_weight[0].T, down_weight[0]
    residual, *pieces, table, gate_up_oth, down_oth = front(
        queries[0], key_rows[0], value_matrix[0], hidden[0].T, norm_gain, out_weight.T,
        block_order, expert_ids[0].T, route_weights[0].T, gate_up_own, down_own,
    )
    return moe(table, pieces, residual, gate_up_own, gate_up_oth, down_own, down_oth).T[None]


def solution(mesh):
    fine = Mesh(mesh.devices.reshape(2, 4, 2, 4, 2), ("y_hi", "x", "y_lo", "z", "core"))
    rows = P(EXP, CTX, None)
    halves = P(CTX + EXP, None, None)
    return jax.shard_map(
        local,
        mesh=fine,
        in_specs=(
            rows, rows, rows, rows, P(CTX, None), P(), P(), rows, rows, halves, halves,
        ),
        out_specs=rows,
        check_vma=False,
    )
```

```python
import functools
import jax
import jax.numpy as jnp
from jax import lax
from jax.experimental import pallas as pl
from jax.experimental.pallas import tpu as pltpu
from jax.sharding import Mesh, PartitionSpec as P

D = 2880
HALF_D = D // 2
HEAD = 64
TOK = 128
QUARTER = 224
Q_FIRST = 112
REST = HALF_D - 4 * QUARTER
AXES = ("y_hi", "x", "y_lo", "z", "core")
MESH = pl.DeviceIdType.MESH
PIECES = ((0, 1024), (1024, 1024), (2048, 832))
CTX = ("y_hi", "x")
EXP = ("y_lo", "z", "core")


def here():
    return {a: lax.axis_index(a) for a in AXES}


def moved(me, axis, by):
    to = dict(me)
    if axis == "y":
        y = (me["y_hi"] * 2 + me["y_lo"] + by) % 4
        to["y_hi"], to["y_lo"] = y // 2, y % 2
    else:
        to[axis] = (me[axis] + by) % 4
    return to


class Copies:
    def __init__(self, send, recv):
        self.send, self.recv, self.made = send, recv, []

    def go(self, src, dst, to):
        i = len(self.made)
        c = pltpu.make_async_remote_copy(
            src_ref=src, dst_ref=dst, send_sem=self.send.at[i], recv_sem=self.recv.at[i],
            device_id=to, device_id_type=MESH,
        )
        c.start()
        self.made.append(c)
        return c

    def drain(self):
        for c in self.made:
            c.wait_send()


def greet(peers):
    barrier = pltpu.get_barrier_semaphore()
    for peer in peers:
        pl.semaphore_signal(barrier, inc=1, device_id=peer, device_id_type=MESH)
    pl.semaphore_wait(barrier, len(peers))


FRONT_COPIES = 80


def front_kernel(
    order, q_in, k_in, v_in, hid_in, gain_in, ow, ids_in, weights_in, gu, dn,
    residual, moe0, moe1, moe2, table, gu_oth, dn_oth,
    q, hid, gain, ids, kv, w, att, acc, got, rows, res_out, m0, m1, m2, tab, send, recv, local_sem,
):
    me = here()
    cp = Copies(send, recv)
    near = []

    def copy(src, dst):
        c = pltpu.make_async_copy(src, dst, local_sem.at[len(near)])
        c.start()
        near.append(c)
        return c

    core = me["core"]
    base = pl.multiple_of(core * HALF_D, 16)
    kv_in = (copy(k_in, kv.at[0, :, pl.ds(0, 256)]), copy(v_in, kv.at[0, :, pl.ds(256, 256)]))
    q_copy = copy(q_in, q)
    ids_copy, weights_copy = copy(ids_in, ids), copy(weights_in, tab.at[pl.ds(4, 4)])
    hid_copy, gain_copy = copy(hid_in, hid), copy(gain_in, gain)
    own_w = copy(ow.at[pl.ds(base, HALF_D)], w.at[0])

    other = dict(me, core=1 - core)
    kv_mate = dict(me, y_hi=1 - me["y_hi"])
    w_mate = dict(me, y_hi=1 - me["y_hi"], y_lo=1 - me["y_lo"])
    xp, xm = moved(me, "x", 1), moved(me, "x", 3)
    zp, zm = moved(me, "z", 1), moved(me, "z", 3)
    z = me["z"]
    greet([other, kv_mate, w_mate, xp, xm, zp, zm])

    def quarter(t, part=None):
        start = REST + QUARTER * ((z + t) % 4)
        size = QUARTER
        if part == 0:
            size = Q_FIRST
        elif part == 1:
            start, size = start + Q_FIRST, QUARTER - Q_FIRST
        return pl.ds(pl.multiple_of(start, 16), size)

    own_q = ow.at[pl.ds(pl.multiple_of(base + REST + QUARTER * z, 16), QUARTER)]
    own_r = ow.at[pl.ds(base, REST)]
    rest = pl.ds(0, REST)
    rest_parts = (pl.ds(0, REST // 2), pl.ds(REST // 2, REST // 2))
    kv_parts = (pl.ds(0, 64), pl.ds(64, 64))
    q_parts = (quarter(0, 0), quarter(0, 1))
    zq, zq2 = {}, {}

    def z_first(slot):
        part = w.at[slot, quarter(0)]
        zq[slot] = (cp.go(part, part, zp), cp.go(part, part, zm))

    def z_second(slot):
        for c in zq[slot]:
            c.wait_recv()
        a, b = w.at[slot, quarter(3, 0)], w.at[slot, quarter(1, 1)]
        zq2[slot] = (cp.go(a, a, zp), cp.go(b, b, zm))

    def x_first(buf, slot, part):
        src = buf.at[slot, part]
        return cp.go(src, buf.at[slot + 3, part], xp), cp.go(src, buf.at[slot + 1, part], xm)

    def x_second(buf, d, firsts, parts):
        for c in firsts:
            c.wait_recv()
        return (
            cp.go(buf.at[4 * d + 3, parts[0]], buf.at[4 * d + 2, parts[0]], xp),
            cp.go(buf.at[4 * d + 1, parts[1]], buf.at[4 * d + 2, parts[1]], xm),
        )

    def arrive(cs):
        for c in cs:
            c.wait_recv()

    yq = cp.go(own_q, w.at[4, quarter(0)], w_mate)
    xq0 = (cp.go(own_q, w.at[3, quarter(0)], xp), cp.go(own_q, w.at[1, quarter(0)], xm))
    for c in kv_in:
        c.wait()
    ky = cp.go(kv.at[0], kv.at[4], kv_mate)
    every = pl.ds(0, TOK)
    kx0 = x_first(kv, 0, every)
    yr = [cp.go(own_r, w.at[4, rest], w_mate)]
    xr = (cp.go(own_r, w.at[3, rest], xp), cp.go(own_r, w.at[1, rest], xm))
    swaps = [cp.go(gu, gu_oth, other), cp.go(dn, dn_oth, other)]
    yq.wait_recv()
    xq1 = x_first(w, 4, quarter(0))
    z_first(4)
    x2q0 = x_second(w, 0, xq0, q_parts)
    z_first(3)
    z_first(1)
    ky.wait_recv()
    kx1 = x_first(kv, 4, every)
    x2q1 = x_second(w, 1, xq1, q_parts)
    z_first(7)
    z_first(5)
    kx20 = x_second(kv, 0, kx0, kv_parts)
    arrive(x2q0)
    z_first(2)
    kx21 = x_second(kv, 1, kx1, kv_parts)
    arrive(x2q1)
    z_first(6)
    z_second(4)
    arrive(yr)
    xr1 = x_first(w, 4, rest)

    ids_copy.wait()
    weights_copy.wait()
    expert = lax.broadcasted_iota(jnp.int32, (64, TOK), 0)
    hits = [ids[k : k + 1, :] == expert for k in range(4)]
    member = jnp.where(hits[0] | hits[1] | hits[2] | hits[3], 1.0, 0.0).astype(jnp.bfloat16)
    earlier = jnp.where(
        lax.broadcasted_iota(jnp.int32, (TOK, TOK), 0) < lax.broadcasted_iota(jnp.int32, (TOK, TOK), 1),
        1.0, 0.0,
    ).astype(jnp.bfloat16)
    place = jnp.dot(member, earlier, preferred_element_type=jnp.float32)
    for k in range(4):
        slot_of = jnp.sum(jnp.where(hits[k], place, 0.0), axis=0, keepdims=True)
        tab[k : k + 1, :] = ids[k : k + 1, :].astype(jnp.float32) * 16.0 + slot_of
    tab_out = copy(tab, table)

    hid_copy.wait()
    for lo in range(0, D, 128):
        n = min(128, D - lo)
        rows[:, lo : lo + n] = hid[lo : lo + n, :].astype(jnp.float32).T

    ctx = me["y_hi"] * 4 + me["x"]
    col = lax.broadcasted_iota(jnp.int32, (1, 1024), 1)
    key_pos = col % 64
    for slot in range(8):
        block = ((me["y_hi"] + slot // 4) % 2) * 4 + (me["x"] + slot % 4) % 4
        for h in (0, 1):
            key_pos = key_pos + jnp.where(
                col // 64 == 2 * slot + h, order[2 * block + h] * 64, 0
            )
    row = lax.broadcasted_iota(jnp.int32, (256, 1), 0) % TOK
    query_pos = row % 64 + jnp.where(row < 64, order[2 * ctx] * 64, order[2 * ctx + 1] * 64)
    bias = jnp.where(key_pos <= query_pos, 0.0, -1e30)
    q_copy.wait()
    arrive(kx20)
    arrive(kx21)

    def group(g):
        keys = kv[:, :, 64 * g : 64 * g + 64].reshape(1024, HEAD)
        values = kv[:, :, 256 + 64 * g : 256 + 64 * g + 64].reshape(1024, HEAD)

        def pair(i, _):
            lanes = pl.ds(pl.multiple_of((4 * g + i) * 128, 128), 128)
            two = q[:, lanes] * jnp.bfloat16(0.125)
            two = jnp.concatenate([two[:, :HEAD], two[:, HEAD:]], axis=0)
            s = lax.dot_general(
                two, keys, (((1,), (1,)), ((), ())), preferred_element_type=jnp.float32
            ) + bias
            p = jnp.exp(s - jnp.max(s, axis=1, keepdims=True))
            total = jnp.sum(p, axis=1, keepdims=True)
            o = jnp.dot(p.astype(jnp.bfloat16), values, preferred_element_type=jnp.float32)
            o = (o / total).astype(jnp.bfloat16)
            att[0, :, lanes] = jnp.concatenate([o[:TOK], o[TOK:]], axis=1)
            return 0

        lax.fori_loop(0, 4, pair, 0)

    group(0)
    x2r0 = x_second(w, 0, xr, rest_parts)
    z_second(3)
    z_second(1)
    group(1)
    z_second(7)
    z_second(5)
    x2r1 = x_second(w, 1, xr1, rest_parts)
    group(2)
    z_second(2)
    z_second(6)
    group(3)
    att_out = cp.go(att.at[0], att.at[1], other)
    own_w.wait()
    att_out.wait_recv()

    def project(slot, first=False):
        block = ((me["y_hi"] + slot // 4) % 2) * 4 + (me["x"] + slot % 4) % 4
        lanes = pl.ds(pl.multiple_of(block * 256, 256), 256)
        both = att[:, :, lanes].reshape(2 * TOK, 256)
        part = lax.dot_general(
            both, w[slot], (((1,), (1,)), ((), ())), preferred_element_type=jnp.float32
        ).reshape(2, TOK, HALF_D)
        acc[...] = part if first else acc[...] + part

    project(0, True)
    for slot in (3, 1, 4, 7, 5, 2, 6):
        arrive(zq2[slot])
        if slot in (2, 6):
            arrive(x2r0 if slot == 2 else x2r1)
        project(slot)
    back = cp.go(acc.at[1], got, other)
    gain_copy.wait()
    back.wait_recv()
    mine, theirs = acc[0], got[...]
    left = jnp.where(core == 0, mine, theirs)
    right = jnp.where(core == 0, theirs, mine)
    res = (rows[...] + jnp.concatenate([left, right], axis=1)).astype(jnp.bfloat16)
    res_out[...] = res
    outs = [copy(res_out, residual)]
    res = res.astype(jnp.float32)
    scale = lax.rsqrt(jnp.mean(res * res, axis=1, keepdims=True) + 1e-05)
    normed = (res * scale * gain[...].reshape(1, D)).astype(jnp.bfloat16)
    for (lo, width), m, o in zip(PIECES, (m0, m1, m2), (moe0, moe1, moe2), strict=True):
        m[...] = normed[:, lo : lo + width]
        outs.append(copy(m, o))
    for c in outs:
        c.wait()
    tab_out.wait()
    arrive(swaps)
    cp.drain()


def front(q, k, v, hidden_t, gain, ow_t, order, ids_t, weights_t, gu_t, dn):
    anyspace = pl.BlockSpec(memory_space=pl.ANY)
    bf = jnp.bfloat16
    pieces = [(TOK, width) for _, width in PIECES]
    return pl.pallas_call(
        front_kernel,
        out_shape=(
            jax.ShapeDtypeStruct((TOK, D), bf),
            *(jax.ShapeDtypeStruct(p, bf) for p in pieces),
            jax.ShapeDtypeStruct((8, TOK), jnp.float32),
            jax.ShapeDtypeStruct(gu_t.shape, bf), jax.ShapeDtypeStruct(dn.shape, bf),
        ),
        in_specs=[pl.BlockSpec(memory_space=pltpu.SMEM)] + [anyspace] * 10,
        out_specs=(anyspace,) * 7,
        scratch_shapes=[
            pltpu.VMEM((TOK, 2048), bf),
            pltpu.VMEM((D, TOK), bf),
            pltpu.VMEM((D,), jnp.float32),
            pltpu.VMEM((4, TOK), jnp.int32),
            pltpu.VMEM((8, TOK, 512), bf),
            pltpu.VMEM((8, HALF_D, 256), bf),
            pltpu.VMEM((2, TOK, 2048), bf),
            pltpu.VMEM((2, TOK, HALF_D), jnp.float32),
            pltpu.VMEM((TOK, HALF_D), jnp.float32),
            pltpu.VMEM((TOK, D), jnp.float32),
            pltpu.VMEM((TOK, D), bf),
            *(pltpu.VMEM(p, bf) for p in pieces),
            pltpu.VMEM((8, TOK), jnp.float32),
            pltpu.SemaphoreType.DMA((FRONT_COPIES,)),
            pltpu.SemaphoreType.DMA((FRONT_COPIES,)),
            pltpu.SemaphoreType.DMA((16,)),
        ],
        compiler_params=pltpu.CompilerParams(
            collective_id=0, has_side_effects=True, vmem_limit_bytes=60 * 2**20
        ),
    )(order, q, k, v, hidden_t, gain, ow_t, ids_t, weights_t, gu_t, dn)


TURNS = (("x", "y", "z"), ("y", "z", "x"), ("z", "x", "y"))
ORDER = (0, 2, 1, 3)
MOE_COPIES = 200
FF_HALF = 720


def moe_kernel(
    table, in0, in1, in2, residual, gu0, gu1, dn0, dn1,
    out, *refs,
):
    r2, q3 = refs[0:3], refs[3:6]
    t, s_buf, r3, q2, tab, part, got = (refs[6 + 3 * i : 9 + 3 * i] for i in range(7))
    gu, dn, act, res, send, recv, local_sem = refs[27:]
    me = here()
    cp = Copies(send, recv)
    near = []

    def copy(src, dst):
        c = pltpu.make_async_copy(src, dst, local_sem.at[len(near)])
        c.start()
        near.append(c)
        return c

    def go(src, dst, axis, by):
        if by == 0:
            return copy(src, dst)
        return cp.go(src, dst, moved(me, axis, by))

    def arrive(cs):
        for c in cs:
            if any(c is n for n in near):
                c.wait()
            else:
                c.wait_recv()

    tab_in = [copy(table, tab[p].at[0]) for p in range(3)]
    own_in = [copy(src, t[p].at[0]) for p, src in enumerate((in0, in1, in2))]
    loads = [copy(gu0, gu.at[0]), copy(gu1, gu.at[1]), copy(dn0, dn.at[0]), copy(dn1, dn.at[1])]
    res_in = copy(residual, res)
    greet([moved(me, a, by) for a in ("x", "y", "z") for by in (1, 3, 2)])

    tabs, ones, twos = {}, {}, {}
    for p in range(3):
        a = TURNS[p][0]
        tab_in[p].wait()
        tabs[p] = [go(tab[p].at[0], tab[p].at[4 - by], a, by) for by in (1, 3, 2)]
    for p in range(3):
        a = TURNS[p][0]
        own_in[p].wait()
        ones[p] = (go(t[p].at[0], t[p].at[3], a, 1), go(t[p].at[0], t[p].at[1], a, 3))

    row = lax.broadcasted_iota(jnp.int32, (256, 1), 0)
    y_me = me["y_hi"] * 2 + me["y_lo"]

    def row_code(p):
        at = {"x": me["x"], "y": y_me, "z": me["z"]}
        _, b, c = TURNS[p]
        at[b] = (at[b] + row // 64) % 4
        at[c] = (at[c] + (row // 16) % 4) % 4
        expert = (at["y"] // 2) * 32 + at["x"] * 8 + (at["y"] % 2) * 4 + at["z"]
        return (expert * 16 + row % 16).astype(jnp.float32)

    def rows_of(bufs, p, s):
        return bufs[p].at[:, :, s] if p < 2 else bufs[p].at[:, s]

    def build(p, s):
        code = row_code(p)
        width = PIECES[p][1]
        hit = tab[p][s, 0:1, :] == code
        for k in range(1, 4):
            hit = hit | (tab[p][s, k : k + 1, :] == code)
        pick = jnp.where(hit, 1.0, 0.0).astype(jnp.bfloat16)
        rows = jnp.dot(pick, t[p][s], preferred_element_type=jnp.float32).astype(jnp.bfloat16)
        rows_of(s_buf, p, s)[...] = rows.reshape(4, 4, 16, width)

    second = {d: [] for d in ORDER}

    def second_two(d):
        for b in (1, 3, 2):
            second[d].append(go(s_buf[2].at[b, d], r2[2].at[4 - b, d], "x", b))

    halves = (pl.ds(0, 64), pl.ds(64, 64))
    for p in range(3):
        a = TURNS[p][0]
        arrive(ones[p])
        twos[p] = (
            go(t[p].at[3, halves[0]], t[p].at[2, halves[0]], a, 1),
            go(t[p].at[1, halves[1]], t[p].at[2, halves[1]], a, 3),
        )
    for p in range(3):
        arrive(tabs[p])
        for s in (0, 3, 1):
            build(p, s)
    for p in range(3):
        arrive(twos[p])
        build(p, 2)
    for d in ORDER:
        c = (4 - d) % 4
        for b in (1, 3, 2):
            second[d].append(go(s_buf[0].at[b, c], r2[0].at[4 - b, c], "y", b))
        second_two(d)
        if d:
            second[d].append(go(s_buf[1].at[4 - d], r2[1].at[d], "z", 4 - d))

    third = {}

    def forward(d):
        arrive(second[d])
        cs = []
        c0 = (4 - d) % 4
        cs.append(go(r2[0].at[pl.ds(1, 3), c0], r3[0].at[d, pl.ds(1, 3)], "z", c0))
        cs.append(go(s_buf[0].at[0, c0], r3[0].at[d, 0], "z", c0))
        for c in (1, 3, 2, 0):
            o = (4 - c) % 4
            src = r2[1].at[d, c] if d else s_buf[1].at[0, c]
            cs.append(go(src, r3[1].at[d, :, o], "x", c))
            cs.append(go(r2[2].at[pl.ds(1, 3), d, c], r3[2].at[d, o, pl.ds(1, 3)], "y", c))
            cs.append(go(s_buf[2].at[0, d, c], r3[2].at[d, o, 0], "y", c))
        third[d] = cs

    back3, back2 = {}, {}

    def give_back(d, p):
        cs, done = [], []
        c0 = (4 - d) % 4
        if p == 0:
            if d:
                cs.append(go(r3[0].at[d, pl.ds(1, 3)], q3[0].at[pl.ds(1, 3), c0], "z", d))
            done.append(go(r3[0].at[d, 0], q2[0].at[0, c0], "z", d))
        for o in (1, 3, 2, 0):
            c = (4 - o) % 4
            if p == 1:
                if d == 0:
                    done.append(go(r3[1].at[d, :, o], q2[1].at[0, c], "x", o))
                elif o:
                    cs.append(go(r3[1].at[d, :, o], q3[1].at[d, c], "x", o))
            elif p == 2:
                if o:
                    cs.append(go(r3[2].at[d, o, pl.ds(1, 3)], q3[2].at[pl.ds(1, 3), d, c], "y", o))
                done.append(go(r3[2].at[d, o, 0], q2[2].at[0, d, c], "y", o))
        back3[p, d] = cs
        back2[p, d] = done

    def hand_on(d):
        c0 = (4 - d) % 4
        arrive(back3[0, d])
        for o in (1, 3, 2):
            src = q3[0].at[o, c0] if d else r3[0].at[0, o]
            back2[0, d].append(go(src, q2[0].at[4 - o, c0], "y", o))
        arrive(back3[1, d])
        if d:
            back2[1, d].append(go(r3[1].at[d, :, 0], q2[1].at[4 - d, 0], "z", d))
            back2[1, d].append(
                go(q3[1].at[d, pl.ds(1, 3)], q2[1].at[4 - d, pl.ds(1, 3)], "z", d)
            )
        arrive(back3[2, d])
        for o in (1, 3, 2):
            b = 4 - o
            back2[2, d].append(go(r3[2].at[d, 0, o], q2[2].at[b, d, 0], "x", o))
            back2[2, d].append(
                go(q3[2].at[o, d, pl.ds(1, 3)], q2[2].at[b, d, pl.ds(1, 3)], "x", o)
            )

    def experts(d):
        arrive(third[d])
        xs = [r3[p][d].reshape(256, PIECES[p][1]) for p in range(3)]

        def first(h, _):
            def side(start):
                total = None
                for p in range(3):
                    lo, width = PIECES[p]
                    y = lax.dot_general(
                        xs[p], gu[h, start : start + FF_HALF, lo : lo + width],
                        (((1,), (1,)), ((), ())), preferred_element_type=jnp.float32,
                    )
                    total = y if total is None else total + y
                return total

            gate, up = side(0), side(FF_HALF)
            act[h] = (gate * (1.0 / (1.0 + jnp.exp(-1.702 * gate))) * (up + 1.0)).astype(jnp.bfloat16)
            return 0

        lax.fori_loop(0, 2, first, 0)
        for p in range(3):
            lo, width = PIECES[p]
            y = jnp.dot(
                act[0], dn[0, :, lo : lo + width], preferred_element_type=jnp.float32
            ) + jnp.dot(act[1], dn[1, :, lo : lo + width], preferred_element_type=jnp.float32)
            r3[p][d] = y.astype(jnp.bfloat16).reshape(4, 4, 16, width)
            give_back(d, p)

    last = []

    def combine(p, s):
        code = row_code(p)
        width = PIECES[p][1]
        spread = jnp.zeros((256, TOK), jnp.float32)
        for k in range(4):
            spread = spread + jnp.where(
                tab[p][s, k : k + 1, :] == code, tab[p][s, 4 + k : 5 + k, :], 0.0
            )
        high = spread.astype(jnp.bfloat16)
        low = (spread - high.astype(jnp.float32)).astype(jnp.bfloat16)
        rows = rows_of(q2, p, s)[...].reshape(256, width)
        over = (((0,), (0,)), ((), ()))
        return lax.dot_general(
            high, rows, over, preferred_element_type=jnp.float32
        ) + lax.dot_general(low, rows, over, preferred_element_type=jnp.float32)

    def hand_in(p, s):
        part[p][s - 1] = combine(p, s).astype(jnp.bfloat16)
        last.append(go(part[p].at[s - 1], got[p].at[3 - s], TURNS[p][0], s))

    forward(0)
    forward(2)
    forward(1)
    forward(3)
    for c in loads:
        c.wait()
    experts(0)
    experts(2)
    hand_on(0)
    experts(1)
    hand_on(2)
    experts(3)
    hand_on(1)
    hand_on(3)
    for p in range(3):
        for d in ORDER:
            arrive(back2[p, d])
    for s in (1, 3, 2):
        for p in range(3):
            hand_in(p, s)
    res_in.wait()
    owns = []
    for p in range(3):
        lo, width = PIECES[p]
        owns.append(res[:, lo : lo + width].astype(jnp.float32) + combine(p, 0))
    for c in last:
        c.wait_recv()
    for p in range(3):
        lo, width = PIECES[p]
        total = owns[p]
        for i in range(3):
            total = total + got[p][i].astype(jnp.float32)
        for at in range(0, width, 128):
            n = min(128, width - at)
            out[lo + at : lo + at + n, :] = total[:, at : at + n].T.astype(jnp.bfloat16)
    cp.drain()


def moe(table, pieces, residual, gu0, gu1, dn0, dn1):
    vmem, anyspace = pl.BlockSpec(memory_space=pltpu.VMEM), pl.BlockSpec(memory_space=pl.ANY)
    bf = jnp.bfloat16
    widths = [w for _, w in PIECES]
    far = [jax.ShapeDtypeStruct((4, 4, 4, 16, w), bf) for w in widths] * 2
    return pl.pallas_call(
        moe_kernel,
        out_shape=(jax.ShapeDtypeStruct((D, TOK), bf), *far),
        in_specs=[anyspace] * 9,
        out_specs=(vmem, *([anyspace] * 6)),
        scratch_shapes=[
            *(pltpu.VMEM((4, TOK, w), bf) for w in widths),
            *(pltpu.VMEM((4, 4, 4, 16, w), bf) for w in widths * 3),
            *(pltpu.VMEM((4, 8, TOK), jnp.float32) for w in widths),
            *(pltpu.VMEM((3, TOK, w), bf) for w in widths),
            *(pltpu.VMEM((3, TOK, w), bf) for w in widths),
            pltpu.VMEM((2, HALF_D, D), bf),
            pltpu.VMEM((2, FF_HALF, D), bf),
            pltpu.VMEM((2, 256, FF_HALF), bf),
            pltpu.VMEM((TOK, D), bf),
            pltpu.SemaphoreType.DMA((MOE_COPIES,)),
            pltpu.SemaphoreType.DMA((MOE_COPIES,)),
            pltpu.SemaphoreType.DMA((64,)),
        ],
        compiler_params=pltpu.CompilerParams(
            collective_id=1, has_side_effects=True, vmem_limit_bytes=60 * 2**20
        ),
    )(table, *pieces, residual, gu0, gu1, dn0, dn1)[0]


def local(
    queries, key_rows, value_matrix, hidden, out_weight, norm_gain, block_order,
    expert_ids, route_weights, gate_up_weight, down_weight,
):
    gate_up_own, down_own = gate_up_weight[0].T, down_weight[0]
    residual, *pieces, table, gate_up_oth, down_oth = front(
        queries[0], key_rows[0], value_matrix[0], hidden[0].T, norm_gain, out_weight.T,
        block_order, expert_ids[0].T, route_weights[0].T, gate_up_own, down_own,
    )
    return moe(table, pieces, residual, gate_up_own, gate_up_oth, down_own, down_oth).T[None]


def solution(mesh):
    fine = Mesh(mesh.devices.reshape(2, 4, 2, 4, 2), ("y_hi", "x", "y_lo", "z", "core"))
    rows = P(EXP, CTX, None)
    halves = P(CTX + EXP, None, None)
    return jax.shard_map(
        local,
        mesh=fine,
        in_specs=(
            rows, rows, rows, rows, P(CTX, None), P(), P(), rows, rows, halves, halves,
        ),
        out_specs=rows,
        check_vma=False,
    )
```

```python
import functools
import jax
import jax.numpy as jnp
from jax import lax
from jax.experimental import pallas as pl
from jax.experimental.pallas import tpu as pltpu
from jax.sharding import Mesh, PartitionSpec as P

D = 2880
HALF_D = D // 2
HEAD = 64
TOK = 128
QUARTER = 224
Q_FIRST = 112
REST = HALF_D - 4 * QUARTER
AXES = ("y_hi", "x", "y_lo", "z", "core")
MESH = pl.DeviceIdType.MESH
PIECES = ((0, 1024), (1024, 1024), (2048, 832))
CTX = ("y_hi", "x")
EXP = ("y_lo", "z", "core")


def here():
    return {a: lax.axis_index(a) for a in AXES}


def moved(me, axis, by):
    to = dict(me)
    if axis == "y":
        y = (me["y_hi"] * 2 + me["y_lo"] + by) % 4
        to["y_hi"], to["y_lo"] = y // 2, y % 2
    else:
        to[axis] = (me[axis] + by) % 4
    return to


class Copies:
    def __init__(self, send, recv):
        self.send, self.recv, self.made = send, recv, []

    def go(self, src, dst, to):
        i = len(self.made)
        c = pltpu.make_async_remote_copy(
            src_ref=src, dst_ref=dst, send_sem=self.send.at[i], recv_sem=self.recv.at[i],
            device_id=to, device_id_type=MESH,
        )
        c.start()
        self.made.append(c)
        return c

    def drain(self):
        for c in self.made:
            c.wait_send()


def greet(peers):
    barrier = pltpu.get_barrier_semaphore()
    for peer in peers:
        pl.semaphore_signal(barrier, inc=1, device_id=peer, device_id_type=MESH)
    pl.semaphore_wait(barrier, len(peers))


FRONT_COPIES = 80


def front_kernel(
    order, q_in, k_in, v_in, hid_in, gain_in, ow, ids_in, weights_in, gu, dn,
    residual, moe0, moe1, moe2, table, gu_oth, dn_oth,
    q, hid, gain, ids, kv, w, att, acc, got, rows, res_out, m0, m1, m2, tab, send, recv, local_sem,
):
    me = here()
    cp = Copies(send, recv)
    near = []

    def copy(src, dst):
        c = pltpu.make_async_copy(src, dst, local_sem.at[len(near)])
        c.start()
        near.append(c)
        return c

    core = me["core"]
    base = pl.multiple_of(core * HALF_D, 16)
    kv_in = (copy(k_in, kv.at[0, :, pl.ds(0, 256)]), copy(v_in, kv.at[0, :, pl.ds(256, 256)]))
    q_copy = copy(q_in, q)
    ids_copy, weights_copy = copy(ids_in, ids), copy(weights_in, tab.at[pl.ds(4, 4)])
    hid_copy, gain_copy = copy(hid_in, hid), copy(gain_in, gain)
    own_w = copy(ow.at[pl.ds(base, HALF_D)], w.at[0])

    other = dict(me, core=1 - core)
    kv_mate = dict(me, y_hi=1 - me["y_hi"])
    w_mate = dict(me, y_hi=1 - me["y_hi"], y_lo=1 - me["y_lo"])
    xp, xm = moved(me, "x", 1), moved(me, "x", 3)
    zp, zm = moved(me, "z", 1), moved(me, "z", 3)
    z = me["z"]
    greet([other, kv_mate, w_mate, xp, xm, zp, zm])

    def quarter(t, part=None):
        start = REST + QUARTER * ((z + t) % 4)
        size = QUARTER
        if part == 0:
            size = Q_FIRST
        elif part == 1:
            start, size = start + Q_FIRST, QUARTER - Q_FIRST
        return pl.ds(pl.multiple_of(start, 16), size)

    own_q = ow.at[pl.ds(pl.multiple_of(base + REST + QUARTER * z, 16), QUARTER)]
    own_r = ow.at[pl.ds(base, REST)]
    rest = pl.ds(0, REST)
    rest_parts = (pl.ds(0, REST // 2), pl.ds(REST // 2, REST // 2))
    kv_parts = (pl.ds(0, 64), pl.ds(64, 64))
    q_parts = (quarter(0, 0), quarter(0, 1))
    zq, zq2 = {}, {}

    def z_first(slot):
        part = w.at[slot, quarter(0)]
        zq[slot] = (cp.go(part, part, zp), cp.go(part, part, zm))

    def z_second(slot):
        for c in zq[slot]:
            c.wait_recv()
        a, b = w.at[slot, quarter(3, 0)], w.at[slot, quarter(1, 1)]
        zq2[slot] = (cp.go(a, a, zp), cp.go(b, b, zm))

    def x_first(buf, slot, part):
        src = buf.at[slot, part]
        return cp.go(src, buf.at[slot + 3, part], xp), cp.go(src, buf.at[slot + 1, part], xm)

    def x_second(buf, d, firsts, parts):
        for c in firsts:
            c.wait_recv()
        return (
            cp.go(buf.at[4 * d + 3, parts[0]], buf.at[4 * d + 2, parts[0]], xp),
            cp.go(buf.at[4 * d + 1, parts[1]], buf.at[4 * d + 2, parts[1]], xm),
        )

    def arrive(cs):
        for c in cs:
            c.wait_recv()

    for c in kv_in:
        c.wait()
    ky = cp.go(kv.at[0], kv.at[4], kv_mate)
    every = pl.ds(0, TOK)
    kx0 = x_first(kv, 0, every)
    yq = cp.go(own_q, w.at[4, quarter(0)], w_mate)
    xq0 = (cp.go(own_q, w.at[3, quarter(0)], xp), cp.go(own_q, w.at[1, quarter(0)], xm))
    yr = [cp.go(own_r, w.at[4, rest], w_mate)]
    xr = (cp.go(own_r, w.at[3, rest], xp), cp.go(own_r, w.at[1, rest], xm))
    swaps = [cp.go(gu, gu_oth, other), cp.go(dn, dn_oth, other)]
    yq.wait_recv()
    xq1 = x_first(w, 4, quarter(0))
    z_first(4)
    x2q0 = x_second(w, 0, xq0, q_parts)
    z_first(3)
    z_first(1)
    ky.wait_recv()
    kx1 = x_first(kv, 4, every)
    x2q1 = x_second(w, 1, xq1, q_parts)
    z_first(7)
    z_first(5)
    kx20 = x_second(kv, 0, kx0, kv_parts)
    arrive(x2q0)
    z_first(2)
    kx21 = x_second(kv, 1, kx1, kv_parts)
    arrive(x2q1)
    z_first(6)
    z_second(4)
    arrive(yr)
    xr1 = x_first(w, 4, rest)

    ids_copy.wait()
    weights_copy.wait()
    expert = lax.broadcasted_iota(jnp.int32, (64, TOK), 0)
    hits = [ids[k : k + 1, :] == expert for k in range(4)]
    member = jnp.where(hits[0] | hits[1] | hits[2] | hits[3], 1.0, 0.0).astype(jnp.bfloat16)
    earlier = jnp.where(
        lax.broadcasted_iota(jnp.int32, (TOK, TOK), 0) < lax.broadcasted_iota(jnp.int32, (TOK, TOK), 1),
        1.0, 0.0,
    ).astype(jnp.bfloat16)
    place = jnp.dot(member, earlier, preferred_element_type=jnp.float32)
    for k in range(4):
        slot_of = jnp.sum(jnp.where(hits[k], place, 0.0), axis=0, keepdims=True)
        tab[k : k + 1, :] = ids[k : k + 1, :].astype(jnp.float32) * 16.0 + slot_of
    tab_out = copy(tab, table)

    hid_copy.wait()
    for lo in range(0, D, 128):
        n = min(128, D - lo)
        rows[:, lo : lo + n] = hid[lo : lo + n, :].astype(jnp.float32).T

    ctx = me["y_hi"] * 4 + me["x"]
    col = lax.broadcasted_iota(jnp.int32, (1, 1024), 1)
    key_pos = col % 64
    for slot in range(8):
        block = ((me["y_hi"] + slot // 4) % 2) * 4 + (me["x"] + slot % 4) % 4
        for h in (0, 1):
            key_pos = key_pos + jnp.where(
                col // 64 == 2 * slot + h, order[2 * block + h] * 64, 0
            )
    row = lax.broadcasted_iota(jnp.int32, (256, 1), 0) % TOK
    query_pos = row % 64 + jnp.where(row < 64, order[2 * ctx] * 64, order[2 * ctx + 1] * 64)
    bias = jnp.where(key_pos <= query_pos, 0.0, -1e30)
    q_copy.wait()
    arrive(kx20)
    arrive(kx21)

    def group(g):
        keys = kv[:, :, 64 * g : 64 * g + 64].reshape(1024, HEAD)
        values = kv[:, :, 256 + 64 * g : 256 + 64 * g + 64].reshape(1024, HEAD)

        def pair(i, _):
            lanes = pl.ds(pl.multiple_of((4 * g + i) * 128, 128), 128)
            two = q[:, lanes] * jnp.bfloat16(0.125)
            two = jnp.concatenate([two[:, :HEAD], two[:, HEAD:]], axis=0)
            s = lax.dot_general(
                two, keys, (((1,), (1,)), ((), ())), preferred_element_type=jnp.float32
            ) + bias
            p = jnp.exp(s - jnp.max(s, axis=1, keepdims=True))
            total = jnp.sum(p, axis=1, keepdims=True)
            o = jnp.dot(p.astype(jnp.bfloat16), values, preferred_element_type=jnp.float32)
            o = (o / total).astype(jnp.bfloat16)
            att[0, :, lanes] = jnp.concatenate([o[:TOK], o[TOK:]], axis=1)
            return 0

        lax.fori_loop(0, 4, pair, 0)

    att_out = []

    def share(g):
        lanes = pl.ds(512 * g, 512)
        att_out.append(cp.go(att.at[0, :, lanes], att.at[1, :, lanes], other))

    group(0)
    share(0)
    x2r0 = x_second(w, 0, xr, rest_parts)
    z_second(3)
    z_second(1)
    group(1)
    share(1)
    z_second(7)
    z_second(5)
    x2r1 = x_second(w, 1, xr1, rest_parts)
    group(2)
    share(2)
    z_second(2)
    z_second(6)
    group(3)
    share(3)
    own_w.wait()
    arrive(att_out)

    def project(slot, first=False):
        block = ((me["y_hi"] + slot // 4) % 2) * 4 + (me["x"] + slot % 4) % 4
        lanes = pl.ds(pl.multiple_of(block * 256, 256), 256)
        both = att[:, :, lanes].reshape(2 * TOK, 256)
        part = lax.dot_general(
            both, w[slot], (((1,), (1,)), ((), ())), preferred_element_type=jnp.float32
        ).reshape(2, TOK, HALF_D)
        acc[...] = part if first else acc[...] + part

    project(0, True)
    for slot in (3, 1, 4, 7, 5, 2, 6):
        arrive(zq2[slot])
        if slot in (2, 6):
            arrive(x2r0 if slot == 2 else x2r1)
        project(slot)
    back = cp.go(acc.at[1], got, other)
    gain_copy.wait()
    back.wait_recv()
    mine, theirs = acc[0], got[...]
    left = jnp.where(core == 0, mine, theirs)
    right = jnp.where(core == 0, theirs, mine)
    res = (rows[...] + jnp.concatenate([left, right], axis=1)).astype(jnp.bfloat16)
    res_out[...] = res
    outs = [copy(res_out, residual)]
    res = res.astype(jnp.float32)
    scale = lax.rsqrt(jnp.mean(res * res, axis=1, keepdims=True) + 1e-05)
    normed = (res * scale * gain[...].reshape(1, D)).astype(jnp.bfloat16)
    for (lo, width), m, o in zip(PIECES, (m0, m1, m2), (moe0, moe1, moe2), strict=True):
        m[...] = normed[:, lo : lo + width]
        outs.append(copy(m, o))
    for c in outs:
        c.wait()
    tab_out.wait()
    arrive(swaps)
    cp.drain()


def front(q, k, v, hidden_t, gain, ow_t, order, ids_t, weights_t, gu_t, dn):
    anyspace = pl.BlockSpec(memory_space=pl.ANY)
    bf = jnp.bfloat16
    pieces = [(TOK, width) for _, width in PIECES]
    return pl.pallas_call(
        front_kernel,
        out_shape=(
            jax.ShapeDtypeStruct((TOK, D), bf),
            *(jax.ShapeDtypeStruct(p, bf) for p in pieces),
            jax.ShapeDtypeStruct((8, TOK), jnp.float32),
            jax.ShapeDtypeStruct(gu_t.shape, bf), jax.ShapeDtypeStruct(dn.shape, bf),
        ),
        in_specs=[pl.BlockSpec(memory_space=pltpu.SMEM)] + [anyspace] * 10,
        out_specs=(anyspace,) * 7,
        scratch_shapes=[
            pltpu.VMEM((TOK, 2048), bf),
            pltpu.VMEM((D, TOK), bf),
            pltpu.VMEM((D,), jnp.float32),
            pltpu.VMEM((4, TOK), jnp.int32),
            pltpu.VMEM((8, TOK, 512), bf),
            pltpu.VMEM((8, HALF_D, 256), bf),
            pltpu.VMEM((2, TOK, 2048), bf),
            pltpu.VMEM((2, TOK, HALF_D), jnp.float32),
            pltpu.VMEM((TOK, HALF_D), jnp.float32),
            pltpu.VMEM((TOK, D), jnp.float32),
            pltpu.VMEM((TOK, D), bf),
            *(pltpu.VMEM(p, bf) for p in pieces),
            pltpu.VMEM((8, TOK), jnp.float32),
            pltpu.SemaphoreType.DMA((FRONT_COPIES,)),
            pltpu.SemaphoreType.DMA((FRONT_COPIES,)),
            pltpu.SemaphoreType.DMA((16,)),
        ],
        compiler_params=pltpu.CompilerParams(
            collective_id=0, has_side_effects=True, vmem_limit_bytes=60 * 2**20
        ),
    )(order, q, k, v, hidden_t, gain, ow_t, ids_t, weights_t, gu_t, dn)


TURNS = (("x", "y", "z"), ("y", "z", "x"), ("z", "x", "y"))
ORDER = (0, 1, 3, 2)
MOE_COPIES = 200
FF_HALF = 720


def moe_kernel(
    table, in0, in1, in2, residual, gu0, gu1, dn0, dn1,
    out, *refs,
):
    r2, q3 = refs[0:3], refs[3:6]
    t, s_buf, r3, q2, tab, part, got = (refs[6 + 3 * i : 9 + 3 * i] for i in range(7))
    gu, dn, act, res, send, recv, local_sem = refs[27:]
    me = here()
    cp = Copies(send, recv)
    near = []

    def copy(src, dst):
        c = pltpu.make_async_copy(src, dst, local_sem.at[len(near)])
        c.start()
        near.append(c)
        return c

    def go(src, dst, axis, by):
        if by == 0:
            return copy(src, dst)
        return cp.go(src, dst, moved(me, axis, by))

    def arrive(cs):
        for c in cs:
            if any(c is n for n in near):
                c.wait()
            else:
                c.wait_recv()

    tab_in = [copy(table, tab[p].at[0]) for p in range(3)]
    own_in = [copy(src, t[p].at[0]) for p, src in enumerate((in0, in1, in2))]
    loads = [copy(gu0, gu.at[0]), copy(gu1, gu.at[1]), copy(dn0, dn.at[0]), copy(dn1, dn.at[1])]
    res_in = copy(residual, res)
    greet([moved(me, a, by) for a in ("x", "y", "z") for by in (1, 3, 2)])

    tabs, ones, twos = {}, {}, {}
    for p in range(3):
        a = TURNS[p][0]
        tab_in[p].wait()
        tabs[p] = [go(tab[p].at[0], tab[p].at[4 - by], a, by) for by in (1, 3, 2)]
    for p in range(3):
        a = TURNS[p][0]
        own_in[p].wait()
        ones[p] = (go(t[p].at[0], t[p].at[3], a, 1), go(t[p].at[0], t[p].at[1], a, 3))

    row = lax.broadcasted_iota(jnp.int32, (256, 1), 0)
    y_me = me["y_hi"] * 2 + me["y_lo"]

    def row_code(p):
        at = {"x": me["x"], "y": y_me, "z": me["z"]}
        _, b, c = TURNS[p]
        at[b] = (at[b] + row // 64) % 4
        at[c] = (at[c] + (row // 16) % 4) % 4
        expert = (at["y"] // 2) * 32 + at["x"] * 8 + (at["y"] % 2) * 4 + at["z"]
        return (expert * 16 + row % 16).astype(jnp.float32)

    def rows_of(bufs, p, s):
        return bufs[p].at[:, :, s] if p < 2 else bufs[p].at[:, s]

    def build(p, s):
        code = row_code(p)
        width = PIECES[p][1]
        hit = tab[p][s, 0:1, :] == code
        for k in range(1, 4):
            hit = hit | (tab[p][s, k : k + 1, :] == code)
        pick = jnp.where(hit, 1.0, 0.0).astype(jnp.bfloat16)
        rows = jnp.dot(pick, t[p][s], preferred_element_type=jnp.float32).astype(jnp.bfloat16)
        rows_of(s_buf, p, s)[...] = rows.reshape(4, 4, 16, width)

    second = {d: [] for d in ORDER}

    def second_two(d):
        for b in (1, 3, 2):
            second[d].append(go(s_buf[2].at[b, d], r2[2].at[4 - b, d], "x", b))

    halves = (pl.ds(0, 64), pl.ds(64, 64))
    for p in range(3):
        a = TURNS[p][0]
        arrive(ones[p])
        twos[p] = (
            go(t[p].at[3, halves[0]], t[p].at[2, halves[0]], a, 1),
            go(t[p].at[1, halves[1]], t[p].at[2, halves[1]], a, 3),
        )
    for p in range(3):
        arrive(tabs[p])
        for s in (0, 3, 1):
            build(p, s)
    for p in range(3):
        arrive(twos[p])
        build(p, 2)
    for d in ORDER:
        c = (4 - d) % 4
        for b in (1, 3, 2):
            second[d].append(go(s_buf[0].at[b, c], r2[0].at[4 - b, c], "y", b))
        second_two(d)
        if d:
            second[d].append(go(s_buf[1].at[4 - d], r2[1].at[d], "z", 4 - d))

    third = {}

    def forward(d):
        arrive(second[d])
        cs = []
        c0 = (4 - d) % 4
        cs.append(go(r2[0].at[pl.ds(1, 3), c0], r3[0].at[d, pl.ds(1, 3)], "z", c0))
        cs.append(go(s_buf[0].at[0, c0], r3[0].at[d, 0], "z", c0))
        for c in (1, 3, 2, 0):
            o = (4 - c) % 4
            src = r2[1].at[d, c] if d else s_buf[1].at[0, c]
            cs.append(go(src, r3[1].at[d, :, o], "x", c))
            cs.append(go(r2[2].at[pl.ds(1, 3), d, c], r3[2].at[d, o, pl.ds(1, 3)], "y", c))
            cs.append(go(s_buf[2].at[0, d, c], r3[2].at[d, o, 0], "y", c))
        third[d] = cs

    back3, back2 = {}, {}

    def give_back(d, p):
        cs, done = [], []
        c0 = (4 - d) % 4
        if p == 0:
            if d:
                cs.append(go(r3[0].at[d, pl.ds(1, 3)], q3[0].at[pl.ds(1, 3), c0], "z", d))
            done.append(go(r3[0].at[d, 0], q2[0].at[0, c0], "z", d))
        for o in (1, 3, 2, 0):
            c = (4 - o) % 4
            if p == 1:
                if d == 0:
                    done.append(go(r3[1].at[d, :, o], q2[1].at[0, c], "x", o))
                elif o:
                    cs.append(go(r3[1].at[d, :, o], q3[1].at[d, c], "x", o))
            elif p == 2:
                if o:
                    cs.append(go(r3[2].at[d, o, pl.ds(1, 3)], q3[2].at[pl.ds(1, 3), d, c], "y", o))
                done.append(go(r3[2].at[d, o, 0], q2[2].at[0, d, c], "y", o))
        back3[p, d] = cs
        back2[p, d] = done

    def hand_on(d):
        c0 = (4 - d) % 4
        arrive(back3[0, d])
        for o in (1, 3, 2):
            src = q3[0].at[o, c0] if d else r3[0].at[0, o]
            back2[0, d].append(go(src, q2[0].at[4 - o, c0], "y", o))
        arrive(back3[1, d])
        if d:
            back2[1, d].append(go(r3[1].at[d, :, 0], q2[1].at[4 - d, 0], "z", d))
            back2[1, d].append(
                go(q3[1].at[d, pl.ds(1, 3)], q2[1].at[4 - d, pl.ds(1, 3)], "z", d)
            )
        arrive(back3[2, d])
        for o in (1, 3, 2):
            b = 4 - o
            back2[2, d].append(go(r3[2].at[d, 0, o], q2[2].at[b, d, 0], "x", o))
            back2[2, d].append(
                go(q3[2].at[o, d, pl.ds(1, 3)], q2[2].at[b, d, pl.ds(1, 3)], "x", o)
            )

    def experts(d):
        arrive(third[d])
        xs = [r3[p][d].reshape(256, PIECES[p][1]) for p in range(3)]

        def first(h, _):
            def side(start):
                total = None
                for p in range(3):
                    lo, width = PIECES[p]
                    y = lax.dot_general(
                        xs[p], gu[h, start : start + FF_HALF, lo : lo + width],
                        (((1,), (1,)), ((), ())), preferred_element_type=jnp.float32,
                    )
                    total = y if total is None else total + y
                return total

            gate, up = side(0), side(FF_HALF)
            act[h] = (gate * (1.0 / (1.0 + jnp.exp(-1.702 * gate))) * (up + 1.0)).astype(jnp.bfloat16)
            return 0

        lax.fori_loop(0, 2, first, 0)
        for p in range(3):
            lo, width = PIECES[p]
            y = jnp.dot(
                act[0], dn[0, :, lo : lo + width], preferred_element_type=jnp.float32
            ) + jnp.dot(act[1], dn[1, :, lo : lo + width], preferred_element_type=jnp.float32)
            r3[p][d] = y.astype(jnp.bfloat16).reshape(4, 4, 16, width)
            give_back(d, p)

    last = []

    def combine(p, s):
        code = row_code(p)
        width = PIECES[p][1]
        spread = jnp.zeros((256, TOK), jnp.float32)
        for k in range(4):
            spread = spread + jnp.where(
                tab[p][s, k : k + 1, :] == code, tab[p][s, 4 + k : 5 + k, :], 0.0
            )
        high = spread.astype(jnp.bfloat16)
        low = (spread - high.astype(jnp.float32)).astype(jnp.bfloat16)
        rows = rows_of(q2, p, s)[...].reshape(256, width)
        over = (((0,), (0,)), ((), ()))
        return lax.dot_general(
            high, rows, over, preferred_element_type=jnp.float32
        ) + lax.dot_general(low, rows, over, preferred_element_type=jnp.float32)

    def hand_in(p, s):
        part[p][s - 1] = combine(p, s).astype(jnp.bfloat16)
        last.append(go(part[p].at[s - 1], got[p].at[3 - s], TURNS[p][0], s))

    forward(0)
    forward(1)
    forward(3)
    forward(2)
    for c in loads:
        c.wait()
    experts(0)
    experts(1)
    hand_on(0)
    experts(3)
    hand_on(1)
    experts(2)
    hand_on(3)
    hand_on(2)
    for p in range(3):
        for d in ORDER:
            arrive(back2[p, d])
        for s in (1, 3, 2):
            hand_in(p, s)
    res_in.wait()
    owns = []
    for p in range(3):
        lo, width = PIECES[p]
        owns.append(res[:, lo : lo + width].astype(jnp.float32) + combine(p, 0))
    for c in last:
        c.wait_recv()
    for p in range(3):
        lo, width = PIECES[p]
        total = owns[p]
        for i in range(3):
            total = total + got[p][i].astype(jnp.float32)
        for at in range(0, width, 128):
            n = min(128, width - at)
            out[lo + at : lo + at + n, :] = total[:, at : at + n].T.astype(jnp.bfloat16)
    cp.drain()


def moe(table, pieces, residual, gu0, gu1, dn0, dn1):
    vmem, anyspace = pl.BlockSpec(memory_space=pltpu.VMEM), pl.BlockSpec(memory_space=pl.ANY)
    bf = jnp.bfloat16
    widths = [w for _, w in PIECES]
    far = [jax.ShapeDtypeStruct((4, 4, 4, 16, w), bf) for w in widths] * 2
    return pl.pallas_call(
        moe_kernel,
        out_shape=(jax.ShapeDtypeStruct((D, TOK), bf), *far),
        in_specs=[anyspace] * 9,
        out_specs=(vmem, *([anyspace] * 6)),
        scratch_shapes=[
            *(pltpu.VMEM((4, TOK, w), bf) for w in widths),
            *(pltpu.VMEM((4, 4, 4, 16, w), bf) for w in widths * 3),
            *(pltpu.VMEM((4, 8, TOK), jnp.float32) for w in widths),
            *(pltpu.VMEM((3, TOK, w), bf) for w in widths),
            *(pltpu.VMEM((3, TOK, w), bf) for w in widths),
            pltpu.VMEM((2, HALF_D, D), bf),
            pltpu.VMEM((2, FF_HALF, D), bf),
            pltpu.VMEM((2, 256, FF_HALF), bf),
            pltpu.VMEM((TOK, D), bf),
            pltpu.SemaphoreType.DMA((MOE_COPIES,)),
            pltpu.SemaphoreType.DMA((MOE_COPIES,)),
            pltpu.SemaphoreType.DMA((64,)),
        ],
        compiler_params=pltpu.CompilerParams(
            collective_id=1, has_side_effects=True, vmem_limit_bytes=60 * 2**20
        ),
    )(table, *pieces, residual, gu0, gu1, dn0, dn1)[0]


def local(
    queries, key_rows, value_matrix, hidden, out_weight, norm_gain, block_order,
    expert_ids, route_weights, gate_up_weight, down_weight,
):
    gate_up_own, down_own = gate_up_weight[0].T, down_weight[0]
    residual, *pieces, table, gate_up_oth, down_oth = front(
        queries[0], key_rows[0], value_matrix[0], hidden[0].T, norm_gain, out_weight.T,
        block_order, expert_ids[0].T, route_weights[0].T, gate_up_own, down_own,
    )
    return moe(table, pieces, residual, gate_up_own, gate_up_oth, down_own, down_oth).T[None]


def solution(mesh):
    fine = Mesh(mesh.devices.reshape(2, 4, 2, 4, 2), ("y_hi", "x", "y_lo", "z", "core"))
    rows = P(EXP, CTX, None)
    halves = P(CTX + EXP, None, None)
    return jax.shard_map(
        local,
        mesh=fine,
        in_specs=(
            rows, rows, rows, rows, P(CTX, None), P(), P(), rows, rows, halves, halves,
        ),
        out_specs=rows,
        check_vma=False,
    )
```
